256 devices in a mesh: section: 8 (over x_lo, y), expert: 32 (over z, x_hi, core).
Axes of the slice: x: 4 (x_hi: 2, x_lo: 2; x = x_hi * 2 + x_lo), y: 4, z: 8, core: 2. Of those that a mesh axis runs over, the one named last changes fastest.
Arguments:
- tokens: bfloat16 [8, 512, 2048], P('section', 'expert'), may hold values from -12 to 12
- expert_ids: int32 [2, 8, 8, 512, 6], P(None, 'section', None, 'expert'), may hold values from 0 to 63, all different within a row; in each aligned block of 16 rows (0 to 15, 16 to 31, ..., all dimensions but the last counted through in order) at most 2 rows name the same one
- norm_gain: float32 [2, 8, 2048], P(None, 'section'), may hold values from 0.5 to 1.5
- router_weight: bfloat16 [2, 8, 2048, 64], P(None, 'section'), may hold values from -0.125 to 0.125
- gate_weight: bfloat16 [2, 8, 32, 2048, 384], P(None, 'section', 'expert'), may hold values from -0.125 to 0.125
- up_weight: bfloat16 [2, 8, 32, 2048, 384], P(None, 'section', 'expert'), may hold values from -0.125 to 0.125
- down_weight: bfloat16 [2, 8, 32, 384, 2048], P(None, 'section', 'expert'), may hold values from -0.4375 to 0.4375
Outputs:
- window_output: bfloat16 [8, 512, 2048], P('section', 'expert')
The draws below stay inside these ranges and needn't reach their ends.
Inputs may be any that keep to these rules, and one draw needn't show every extreme that they name: `expert_ids`: each row names 6 different experts. Within the 16 rows of one device for one layer and one microbatch, no expert is named by more than 2 rows, and in some such block one expert is named by exactly 2 rows.
All inputs are finite; a program needn't handle non-finite values.
Results may differ from the reference program's by a relative error of at most 0.02.
Values may be sent and summed in bfloat16 or wider, within the bound.
A program may use at most 64 MiB of HBM per device.

```python
import math
import jax
import jax.numpy as jnp
import numpy as np
from jax import lax

D = 2048
FF_H = 384
EXPERTS = 64
TOP = 6
ROWS = 16
MICRO = 8
HELD = 16
TOKENS = 512
CAP = 2
N_SECTION = 8


def draw_tokens(key, part):
    subkeys = jax.random.split(key, 3)
    full_shape = (MICRO, TOKENS, D)
    base_noise = jax.random.normal(subkeys[0], full_shape, jnp.float32)
    row_scale = jnp.exp(jax.random.uniform(subkeys[1], (MICRO, TOKENS, 1), jnp.float32, math.log(0.3), math.log(3.0)))
    column_scale = jnp.exp(jax.random.uniform(subkeys[2], (1, 1, D), jnp.float32, math.log(0.3), math.log(3.0)))
    return jnp.clip(base_noise * row_scale * column_scale, -12.0, 12.0).astype(jnp.bfloat16)


def level_of(key, extent, pieces, smallest, top_value):
    factor_of, own = 1.0, jax.random.fold_in(key, 6)
    for axis_at, blocks in pieces:
        draws = jnp.exp(jax.random.uniform(jax.random.fold_in(own, axis_at), (blocks,), jnp.float32, smallest / len(pieces), top_value / len(pieces)))
        factor_of = factor_of * jnp.repeat(draws, extent[axis_at] // blocks).reshape([-1 if axis == axis_at else 1 for axis in range(len(extent))])
    return factor_of


def assign_block(stream_key, own, number, rows, amount, top, bound, skew):
    sequence = jax.random.permutation(stream_key, amount)
    packed, usual = portions_of(amount, rows * top, bound, skew, True), portions_of(amount, rows * top, bound, skew, False)
    places = jnp.arange(amount)

    def named(tallies, turn):
        used = int((tallies > 0).sum())
        fixed = max(1, used // 4)
        passed = fixed + (places - fixed + turn * (used - fixed)) % max(1, amount - fixed)
        return jnp.zeros((amount,), jnp.int32).at[sequence[jnp.where(places < fixed, places, passed)]].set(jnp.asarray(tallies, jnp.int32))

    tallies = jnp.where(number % 4 == 0, named(packed, number // 4), named(usual, number - number // 4 - 1))
    mixed = jax.random.permutation(jax.random.fold_in(own, 3), amount)
    donor, taker = mixed[0:amount // 2 * 2:2], mixed[1:amount // 2 * 2:2]
    room = jnp.minimum(tallies[donor] - 1, bound - tallies[taker]) // 2
    room = jnp.where((donor == sequence[0]) | (taker == sequence[0]) | (tallies[taker] == 0), 0, jnp.maximum(room, 0))
    passed = jax.random.randint(jax.random.fold_in(own, 4), (amount // 2,), 0, 1 << 20) % (room + 1)
    tallies = tallies.at[donor].add(-passed).at[taker].add(passed)
    items = jnp.searchsorted(jnp.cumsum(tallies), jnp.arange(rows * top), side="right").astype(jnp.int32)
    listing = items.reshape(top, rows).T
    listing = listing[jax.random.permutation(jax.random.fold_in(own, 1), rows)]
    turn = jax.random.randint(jax.random.fold_in(own, 2), (rows, 1), 0, top)
    return jnp.take_along_axis(listing, (jnp.arange(top)[None, :] + turn) % top, axis=1)


def portions_of(count, total, most, skew, full):
    loads = [(1 << 20) // math.isqrt(standing ** skew) + 1 for standing in range(1, count + 1)]
    largest = most if full else min(most, max(-(-total // count), total * loads[0] // sum(loads)))
    least = 1 if total - largest >= count - 1 else 0
    given, surplus = [largest] + [least] * (count - 1), total - largest - least * (count - 1)
    while surplus > 0:
        movable = [i for i in range(1, count) if given[i] < largest] or [i for i in range(1, count) if given[i] < most]
        pool, remaining = sum([loads[i] for i in movable]), surplus
        for i in movable:
            more = min(most - given[i], max(1, remaining * loads[i] // pool), surplus)
            given[i] = given[i] + more
            surplus = surplus - more
    return np.array(given)


def noise(stream_key, extent, scale, reach, shards=(), held_as=jnp.bfloat16):
    drawn = scale * jax.random.normal(stream_key, extent, jnp.float32)
    if shards:
        drawn = drawn * level_of(stream_key, extent, shards, -0.22, 0.18)
    return jnp.clip(drawn, -reach, reach).astype(held_as)


def setup_inputs(seed: int = 0) -> dict:
    keys = jax.random.split(jax.random.key(seed), 8)
    tokens = draw_tokens(jax.random.fold_in(keys[7], 71), 0)
    expert_ids_keys = jax.random.split(jax.random.fold_in(keys[1], 1), 2 * N_SECTION * MICRO * TOKENS // ROWS)
    expert_ids_turns = jax.random.permutation(jax.random.fold_in(keys[1], 3), 2 * N_SECTION * MICRO * TOKENS // ROWS)
    expert_ids = jax.vmap(lambda own, number: assign_block(jax.random.fold_in(keys[1], 2), own, number, ROWS, EXPERTS, TOP, CAP, 2))(expert_ids_keys, expert_ids_turns).reshape((2, N_SECTION, MICRO, TOKENS, TOP))
    norm_gain = jnp.clip(0.5 + 1.0 * jax.random.uniform(keys[2], (2, N_SECTION, D), jnp.float32) ** level_of(keys[2], (2, N_SECTION, D), ((1, 8),), -0.2, 0.2), 0.5, 1.5)
    router_weight = noise(keys[3], (2, N_SECTION, D, EXPERTS), D ** -0.5, 0.125, ((1, 8),))
    gate_weight = noise(keys[4], (2, N_SECTION, 2 * HELD, D, FF_H), D ** -0.5, 0.125, ((1, 8), (2, 32)))
    up_weight = noise(keys[5], (2, N_SECTION, 2 * HELD, D, FF_H), D ** -0.5, 0.125, ((1, 8), (2, 32)))
    down_weight = noise(keys[6], (2, N_SECTION, 2 * HELD, FF_H, D), (FF_H // 2) ** -0.5, 0.4375, ((1, 8), (2, 32)))
    return {"tokens": tokens, "expert_ids": expert_ids, "norm_gain": norm_gain, "router_weight": router_weight, "gate_weight": gate_weight, "up_weight": up_weight, "down_weight": down_weight}


norm_epsilon = 1e-06

def moe_layer(stream_in, ids_now, gain_row, router_now, gate_pieces, up_pieces, down_pieces):
    stream = stream_in.astype(jnp.float32)
    features = stream.shape[1]
    mean_square = lax.optimization_barrier(jnp.mean(stream * stream, axis=-1, keepdims=True))
    normed = (stream * lax.rsqrt(mean_square + norm_epsilon) * gain_row).astype(jnp.bfloat16)
    logits = jnp.dot(normed, router_now, preferred_element_type=jnp.float32)
    picked = jnp.take_along_axis(logits, ids_now, axis=1)
    scores = jax.nn.sigmoid(picked)
    gate_share = scores / lax.optimization_barrier(jnp.sum(scores, axis=1, keepdims=True))
    held_count = gate_pieces.shape[0] // 2
    blocks = ids_now.shape[0] // ROWS
    onehot = (ids_now[:, :, None] == jnp.arange(held_count, dtype=jnp.int32)).astype(jnp.int32)
    pairs = onehot.reshape(blocks, ROWS * TOP, held_count)
    rank_in = jnp.cumsum(pairs, axis=1) - pairs
    slot_of = lax.optimization_barrier(jnp.sum(rank_in * pairs, axis=2)).reshape(ids_now.shape)
    block_of = (jnp.arange(ids_now.shape[0], dtype=jnp.int32) // ROWS)[:, None]
    dump_row = held_count * blocks * CAP
    position = jnp.where(ids_now < held_count, (ids_now * blocks + block_of) * CAP + slot_of, dump_row).astype(jnp.int32)
    gathered = jnp.zeros((dump_row + 1, features), jnp.bfloat16).at[position.reshape(-1)].set(jnp.repeat(normed, TOP, axis=0))
    rows_all = gathered[:dump_row].reshape(held_count, blocks * CAP, features)

    def serve_rows(members):
        rows_one, gate_two, up_two, down_two = members
        summed = jnp.zeros((rows_one.shape[0], features), jnp.float32)
        for half_index in range(2):
            gate_act = jnp.dot(rows_one, gate_two[half_index], preferred_element_type=jnp.float32)
            up_act = jnp.dot(rows_one, up_two[half_index], preferred_element_type=jnp.float32)
            hidden = (jax.nn.silu(gate_act) * up_act).astype(jnp.bfloat16)
            partial_out = jnp.dot(hidden, down_two[half_index], preferred_element_type=jnp.float32).astype(jnp.bfloat16)
            summed = summed + partial_out.astype(jnp.float32)
        return summed.astype(jnp.bfloat16)
    outputs = lax.map(serve_rows, (rows_all, gate_pieces.reshape(held_count, 2, features, -1), up_pieces.reshape(held_count, 2, features, -1), down_pieces.reshape(held_count, 2, -1, features)))
    outputs = lax.optimization_barrier(outputs).astype(jnp.float32)
    padded = jnp.concatenate([outputs.reshape(dump_row, features), jnp.zeros((1, features), jnp.float32)], axis=0)
    values = padded[position]
    branch_sum = lax.optimization_barrier(jnp.sum(gate_share[:, :, None] * values, axis=1))
    return (stream + branch_sum).astype(jnp.bfloat16)

def reference(tokens, expert_ids, norm_gain, router_weight, gate_weight, up_weight, down_weight):

    def run_micro(members):
        stream_now, id_micro = members
        for virtual in range(2):
            for section_index in range(N_SECTION):
                stream_now = moe_layer(stream_now, id_micro[virtual, section_index], norm_gain[virtual, section_index], router_weight[virtual, section_index], gate_weight[virtual, section_index], up_weight[virtual, section_index], down_weight[virtual, section_index])
        return stream_now
    return lax.map(run_micro, (tokens, jnp.moveaxis(expert_ids, 2, 0)))
```

```python
import functools

import jax
import jax.numpy as jnp
from jax import lax
from jax.experimental import pallas as pl
from jax.experimental.pallas import tpu as pltpu
from jax.sharding import PartitionSpec as P

CAP = 2
norm_epsilon = 1e-06

STRIDE = 1
LAG = 0

MESH = pl.DeviceIdType.MESH
LANES = 128
EXPERT_LANE = 64


def relay_kernel(
    sections,
    held,
    tokens_ref,
    mask_ref,
    choose_ref,
    router_ref,
    gain_ref,
    gate_hbm,
    up_hbm,
    down_hbm,
    out_ref,
    gate_up,
    down,
    inbox,
    stage,
    final,
    row_send,
    row_recv,
    pair_recv,
    half_send,
    half_recv,
    back_send,
    back_recv,
    stream_send,
    stream_recv,
    share_send,
    share_recv,
    weight_sem,
    inbox_send_sem,
    inbox_sem,
    stage_sem,
    final_sem,
    row_send_sem,
    row_sem,
    pair_send_sem,
    pair_sem,
    half_send_sem,
    half_sem,
    back_send_sem,
    back_sem,
    stream_send_sem,
    stream_sem,
    share_send_sem,
    share_sem,
):
    section = lax.axis_index("section")
    place = lax.axis_index("expert")
    mine = lax.div(place, 2)
    core = lax.rem(place, 2)
    following = lax.rem(section + 1, sections)
    sibling = mine * 2 + 1 - core
    rows = tokens_ref.shape[0]
    slots = held * CAP
    ff = gate_hbm.shape[2]
    near_slots = row_recv.shape[0]
    far_slots = back_recv.shape[0]
    pass_length = STRIDE * sections
    last_layer = sections - 1 + STRIDE * (2 * sections - 1)
    last_combine = sections - 1 + STRIDE * 2 * sections

    def flat(value):
        return value.reshape(slots, value.shape[-1])

    def blocks(value):
        return value.astype(jnp.bfloat16).reshape(held, CAP, value.shape[-1])

    def other(step):
        return lax.rem(mine + step, held)

    def settle(ref, sem):
        pltpu.make_async_copy(ref, ref, sem).wait()

    loads = []
    for virtual in range(2):
        loads.append(
            [
                pltpu.make_async_copy(
                    gate_hbm.at[virtual],
                    gate_up.at[virtual, :, pl.ds(0, ff)],
                    weight_sem.at[virtual, 0],
                ),
                pltpu.make_async_copy(
                    up_hbm.at[virtual],
                    gate_up.at[virtual, :, pl.ds(ff, ff)],
                    weight_sem.at[virtual, 1],
                ),
                pltpu.make_async_copy(
                    down_hbm.at[virtual], down.at[virtual], weight_sem.at[virtual, 2]
                ),
            ]
        )
        for load in loads[-1]:
            load.start()

    barrier = pltpu.get_barrier_semaphore()
    greeted = 0

    def greet(to_section, to_place):
        pl.semaphore_signal(
            barrier, inc=1, device_id=(to_section, to_place), device_id_type=MESH
        )

    for ahead in range(sections):
        to_section = lax.rem(section + ahead, sections)
        if ahead in (0, 1, sections - 1):
            first = 1 if ahead == 0 else 0

            def greet_step(step, carry, to_section=to_section):
                greet(to_section, other(step) * 2 + core)
                return carry

            lax.fori_loop(first, held, greet_step, 0)
            greeted += held - first
        else:
            greet(to_section, place)
            greeted += 1
    greet(section, sibling)
    pl.semaphore_wait(barrier, greeted + 1)

    def inbox_copy(index):
        return pltpu.make_async_remote_copy(
            tokens_ref,
            inbox.at[index],
            inbox_send_sem,
            inbox_sem.at[index],
            device_id=(0, place),
            device_id_type=MESH,
        )

    def stage_copy(index):
        return pltpu.make_async_remote_copy(
            stage.at[index],
            final,
            stage_sem.at[index],
            final_sem,
            device_id=(index, place),
            device_id_type=MESH,
        )

    @pl.when(section > 0)
    def _():
        inbox_copy(section).start()

    inbox[0] = tokens_ref[...]

    def virtual_of(step):
        return jnp.where(step - STRIDE * section >= pass_length, 1, 0)

    def home(now):
        far = lax.rem(now, far_slots)
        near = lax.rem(now, near_slots)
        two = lax.rem(now, 2)
        target = lax.rem(now + STRIDE, far_slots)

        @pl.when(now >= STRIDE)
        def _():
            settle(stream_recv.at[far], stream_sem.at[far])
            settle(share_recv.at[far], share_sem.at[far])
            settle(back_recv.at[far], back_sem.at[far])

        added = jnp.dot(
            share_recv[far][:, :slots], flat(back_recv[far]), preferred_element_type=jnp.float32
        )
        summed = stream_recv[far].astype(jnp.float32) + (added[:rows] + added[rows:])
        summed = summed.astype(jnp.bfloat16)

        @pl.when((section == 0) & (now >= 2 * pass_length))
        def _():
            index = now - 2 * pass_length

            @pl.when(index == 0)
            def _():
                final[...] = summed

            @pl.when(index > 0)
            def _():
                stage[index] = summed
                stage_copy(index).start()

        @pl.when(now <= last_layer)
        def _():
            starts = (section == 0) & (now < sections)

            @pl.when(starts & (now > 0))
            def _():
                settle(inbox.at[now], inbox_sem.at[now])

            source = jnp.where(starts, now, 0)
            current = jnp.where(starts | (now < STRIDE), inbox[source], summed)

            @pl.when(now >= 2)
            def _():
                settle(stream_send.at[two], stream_send_sem.at[two])
                settle(share_send.at[two], share_send_sem.at[two])
                settle(row_send.at[two, pl.ds(0, held - 1)], row_send_sem.at[two])

            virtual = virtual_of(now)
            offset = now - STRIDE * section - virtual * pass_length
            micro = jnp.minimum(jnp.maximum(offset, 0), sections - 1)
            table = virtual * sections + micro

            stream = current.astype(jnp.float32)
            mean_square = jnp.mean(stream * stream, axis=-1, keepdims=True)
            normed = stream * lax.rsqrt(mean_square + norm_epsilon) * gain_ref[virtual]
            normed = normed.astype(jnp.bfloat16)
            row_send[two] = blocks(
                jnp.dot(choose_ref[table], normed, preferred_element_type=jnp.float32)
            )

            def send_rows(step, carry):
                to = other(step)
                pltpu.make_async_remote_copy(
                    row_send.at[two, to],
                    row_recv.at[near, mine],
                    row_send_sem.at[two],
                    row_sem.at[near],
                    device_id=(section, to * 2 + core),
                    device_id_type=MESH,
                ).start()
                return carry

            lax.fori_loop(1, held, send_rows, 0)
            pltpu.make_async_copy(
                row_send.at[two, mine],
                row_recv.at[near, mine],
                row_sem.at[near],
            ).start()

            stream_send[two] = current
            pltpu.make_async_remote_copy(
                stream_send.at[two],
                stream_recv.at[target],
                stream_send_sem.at[two],
                stream_sem.at[target],
                device_id=(following, place),
                device_id_type=MESH,
            ).start()

            logits = jnp.dot(normed, router_ref[virtual], preferred_element_type=jnp.float32)
            scores = mask_ref[table] / (1.0 + jnp.exp(-logits))
            lane = lax.broadcasted_iota(jnp.int32, scores.shape, 1)
            total = jnp.sum(
                jnp.where(lane >= EXPERT_LANE, scores, 0.0), axis=1, keepdims=True
            )
            share = jnp.where(lane < slots, scores / total, 0.0)
            high = share.astype(jnp.bfloat16)
            low = (share - high.astype(jnp.float32)).astype(jnp.bfloat16)
            share_send[two] = jnp.concatenate([high, low], axis=0)
            pltpu.make_async_remote_copy(
                share_send.at[two],
                share_recv.at[target],
                share_send_sem.at[two],
                share_sem.at[target],
                device_id=(following, place),
                device_id_type=MESH,
            ).start()

    def serve(step):
        near = lax.rem(step, near_slots)
        two = lax.rem(step, 2)
        target = lax.rem(step + STRIDE, far_slots)
        virtual = virtual_of(step)

        settle(row_recv.at[near], row_sem.at[near])
        forward = pltpu.make_async_remote_copy(
            row_recv.at[near],
            pair_recv.at[two],
            pair_send_sem.at[two],
            pair_sem.at[two],
            device_id=(section, sibling),
            device_id_type=MESH,
        )
        forward.start()
        for early in range(2):

            @pl.when(step == early)
            def _(early=early):
                for load in loads[early]:
                    load.wait()

        forward.wait()

        given = jnp.concatenate([flat(row_recv[near]), flat(pair_recv[two])], axis=0)
        both = jnp.dot(given, gate_up[virtual], preferred_element_type=jnp.float32)
        gate_act, up_act = both[:, :ff], both[:, ff:]
        hidden = (gate_act / (1.0 + jnp.exp(-gate_act)) * up_act).astype(jnp.bfloat16)

        half_send[two] = jnp.dot(
            hidden[slots:], down[virtual], preferred_element_type=jnp.float32
        ).astype(jnp.bfloat16)
        half = pltpu.make_async_remote_copy(
            half_send.at[two],
            half_recv.at[two],
            half_send_sem.at[two],
            half_sem.at[two],
            device_id=(section, sibling),
            device_id_type=MESH,
        )
        half.start()
        own = jnp.dot(hidden[:slots], down[virtual], preferred_element_type=jnp.float32)
        own = own.astype(jnp.bfloat16).astype(jnp.float32)

        @pl.when(step >= 2)
        def _():
            settle(back_send.at[two], back_send_sem.at[two])

        half.wait()
        back_send[two] = blocks(own + half_recv[two].astype(jnp.float32))

        def send_back(turn, carry):
            to = other(turn)
            pltpu.make_async_remote_copy(
                back_send.at[two, to],
                back_recv.at[target, mine],
                back_send_sem.at[two],
                back_sem.at[target],
                device_id=(following, to * 2 + core),
                device_id_type=MESH,
            ).start()
            return carry

        lax.fori_loop(0, held, send_back, 0)

    def iteration(now, carry):
        home(now)
        if LAG:

            @pl.when((now >= LAG) & (now <= last_layer + LAG))
            def _():
                serve(now - LAG)

        else:

            @pl.when(now <= last_layer)
            def _():
                serve(now)

        return carry

    lax.fori_loop(0, last_combine + 1, iteration, 0)

    for last in range(2):
        settle(stream_send.at[last], stream_send_sem.at[last])
        settle(share_send.at[last], share_send_sem.at[last])
        settle(row_send.at[last, pl.ds(0, held - 1)], row_send_sem.at[last])
        settle(back_send.at[last], back_send_sem.at[last])

    @pl.when(section > 0)
    def _():
        settle(tokens_ref, inbox_send_sem)
        settle(final, final_sem)

    @pl.when(section == 0)
    def _():
        for index in range(1, sections):
            settle(stage.at[index], stage_sem.at[index])

    out_ref[...] = final[...]


def tables(ids, held):
    rows = ids.shape[-2]
    lane = jnp.arange(LANES, dtype=jnp.int32)
    slots = held * CAP
    meaning = jnp.where(
        lane < slots, lane // CAP, jnp.where(lane >= EXPERT_LANE, lane - EXPERT_LANE, -1)
    )
    named = jnp.any(ids[..., None] == meaning, axis=-2).astype(jnp.float32)
    row = jnp.arange(rows)
    earlier = (row[:, None] > row[None, :]).astype(jnp.float32)
    rank = jnp.sum(earlier[:, :, None] * named[:, None, :, :], axis=2)
    fits = (lane >= slots) | (rank == (lane % CAP).astype(jnp.float32))
    mask = named * fits.astype(jnp.float32)
    choose = jnp.swapaxes(mask[..., :slots], 1, 2).astype(jnp.bfloat16)
    return mask, choose


def body(tokens, expert_ids, norm_gain, router_weight, gate_weight, up_weight, down_weight):
    sections = lax.axis_size("section")
    held = lax.axis_size("expert") // 2
    rows, features = tokens.shape[1:]
    ff = gate_weight.shape[-1]
    slots = held * CAP
    experts = router_weight.shape[-1]
    mask, choose = tables(
        expert_ids[:, 0].reshape(-1, rows, expert_ids.shape[-1]), held
    )
    lane = jnp.arange(LANES, dtype=jnp.int32)
    meaning = jnp.where(
        lane < slots, lane // CAP, jnp.where(lane >= EXPERT_LANE, lane - EXPERT_LANE, -1)
    )
    spread = (jnp.arange(experts)[:, None] == meaning[None, :]).astype(jnp.bfloat16)
    router = jnp.dot(
        router_weight[:, 0], spread, preferred_element_type=jnp.float32
    ).astype(jnp.bfloat16)

    near_slots = 2 + 2 * LAG
    far_slots = STRIDE * sections - LAG + 1
    bf16 = jnp.bfloat16
    dma = pltpu.SemaphoreType.DMA
    vmem = pl.BlockSpec(memory_space=pltpu.VMEM)
    anywhere = pl.BlockSpec(memory_space=pl.ANY)
    out = pl.pallas_call(
        functools.partial(relay_kernel, sections, held),
        out_shape=jax.ShapeDtypeStruct((rows, features), bf16),
        in_specs=[vmem] * 5 + [anywhere] * 3,
        out_specs=vmem,
        scratch_shapes=[
            pltpu.VMEM((2, features, 2 * ff), bf16),
            pltpu.VMEM((2, ff, features), bf16),
            pltpu.VMEM((sections, rows, features), bf16),
            pltpu.VMEM((sections, rows, features), bf16),
            pltpu.VMEM((rows, features), bf16),
            pltpu.VMEM((2, held, CAP, features), bf16),
            pltpu.VMEM((near_slots, held, CAP, features), bf16),
            pltpu.VMEM((2, held, CAP, features), bf16),
            pltpu.VMEM((2, slots, features), bf16),
            pltpu.VMEM((2, slots, features), bf16),
            pltpu.VMEM((2, held, CAP, features), bf16),
            pltpu.VMEM((far_slots, held, CAP, features), bf16),
            pltpu.VMEM((2, rows, features), bf16),
            pltpu.VMEM((far_slots, rows, features), bf16),
            pltpu.VMEM((2, 2 * rows, LANES), bf16),
            pltpu.VMEM((far_slots, 2 * rows, LANES), bf16),
            dma((2, 3)),
            dma,
            dma((sections,)),
            dma((sections,)),
            dma,
            dma((2,)),
            dma((near_slots,)),
            dma((2,)),
            dma((2,)),
            dma((2,)),
            dma((2,)),
            dma((2,)),
            dma((far_slots,)),
            dma((2,)),
            dma((far_slots,)),
            dma((2,)),
            dma((far_slots,)),
        ],
        compiler_params=pltpu.CompilerParams(
            collective_id=0, has_side_effects=True, vmem_limit_bytes=48 << 20
        ),
        name="relay",
    )(
        tokens[0],
        mask,
        choose,
        router,
        norm_gain.reshape(2, 1, features),
        gate_weight[:, 0, 0],
        up_weight[:, 0, 0],
        down_weight[:, 0, 0],
    )
    return out[None]


def solution(mesh):
    return jax.shard_map(
        body,
        mesh=mesh,
        in_specs=(
            P("section", "expert", None),
            P(None, "section", None, "expert", None),
            P(None, "section", None),
            P(None, "section", None, None),
            P(None, "section", "expert", None, None),
            P(None, "section", "expert", None, None),
            P(None, "section", "expert", None, None),
        ),
        out_specs=P("section", "expert", None),
        check_vma=False,
    )
```

```python
import functools

import jax
import jax.numpy as jnp
from jax import lax
from jax.experimental import pallas as pl
from jax.experimental.pallas import tpu as pltpu
from jax.sharding import PartitionSpec as P

CAP = 2
norm_epsilon = 1e-06

LAG = 1

MESH = pl.DeviceIdType.MESH
LANES = 128
EXPERT_LANE = 64


def relay_kernel(
    sections,
    held,
    tokens_ref,
    mask_ref,
    choose_ref,
    router_ref,
    gain_ref,
    gate_hbm,
    up_hbm,
    down_hbm,
    out_ref,
    gate_up,
    down,
    inbox,
    stage,
    final,
    row_send,
    row_recv,
    pair_recv,
    half_send,
    half_recv,
    back_send,
    back_recv,
    stream_send,
    stream_recv,
    share_send,
    share_recv,
    weight_sem,
    inbox_send_sem,
    inbox_sem,
    stage_sem,
    final_sem,
    row_send_sem,
    row_sem,
    pair_send_sem,
    pair_sem,
    half_send_sem,
    half_sem,
    back_send_sem,
    back_sem,
    stream_send_sem,
    stream_sem,
    share_send_sem,
    share_sem,
):
    section = lax.axis_index("section")
    place = lax.axis_index("expert")
    mine = lax.div(place, 2)
    core = lax.rem(place, 2)
    level, side = lax.div(mine, 2), lax.rem(mine, 2)
    levels = held // 2
    last_section = sections - 1
    is_last = section == last_section
    following = lax.rem(section + 1, sections)
    sibling = mine * 2 + 1 - core
    rows = tokens_ref.shape[0]
    slots = held * CAP
    ff = gate_hbm.shape[2]

    def flat(value):
        return value.reshape(slots, value.shape[-1])

    def blocks(value):
        return value.astype(jnp.bfloat16).reshape(held, CAP, value.shape[-1])

    farthest = sorted(
        ((up, across) for up in range(levels) for across in (1, 0)),
        key=lambda move: (-min(move[0], levels - move[0]), -move[1]),
    )

    def chip(move):
        up, across = move
        beside = 1 - side if across else side
        return lax.rem(level + up, levels) * 2 + beside

    def settle(ref, sem):
        pltpu.make_async_copy(ref, ref, sem).wait()

    loads = []
    for virtual in range(2):
        loads.append(
            [
                pltpu.make_async_copy(
                    gate_hbm.at[virtual],
                    gate_up.at[virtual, :, pl.ds(0, ff)],
                    weight_sem.at[virtual, 0],
                ),
                pltpu.make_async_copy(
                    up_hbm.at[virtual],
                    gate_up.at[virtual, :, pl.ds(ff, ff)],
                    weight_sem.at[virtual, 1],
                ),
                pltpu.make_async_copy(
                    down_hbm.at[virtual], down.at[virtual], weight_sem.at[virtual, 2]
                ),
            ]
        )
        for load in loads[-1]:
            load.start()

    barrier = pltpu.get_barrier_semaphore()
    greeted = 0

    def greet(to_section, to_place):
        pl.semaphore_signal(
            barrier, inc=1, device_id=(to_section, to_place), device_id_type=MESH
        )

    for ahead in range(sections):
        to_section = lax.rem(section + ahead, sections)
        if ahead in (0, 1, sections - 1):
            first = 1 if ahead == 0 else 0

            def greet_step(step, carry, to_section=to_section):
                greet(to_section, lax.rem(mine + step, held) * 2 + core)
                return carry

            lax.fori_loop(first, held, greet_step, 0)
            greeted += held - first
        else:
            greet(to_section, place)
            greeted += 1
    greet(section, sibling)
    pl.semaphore_wait(barrier, greeted + 1)

    def inbox_copy(index):
        return pltpu.make_async_remote_copy(
            tokens_ref,
            inbox.at[index],
            inbox_send_sem,
            inbox_sem.at[index],
            device_id=(0, place),
            device_id_type=MESH,
        )

    @pl.when(section > 0)
    def _():
        inbox_copy(section).start()

    @pl.when(section == 0)
    def _():
        inbox[0] = tokens_ref[...]

    def combined(slot):
        added = jnp.dot(
            share_recv[slot][:, :slots],
            flat(back_recv[slot]),
            preferred_element_type=jnp.float32,
        )
        summed = stream_recv[slot].astype(jnp.float32) + (added[:rows] + added[rows:])
        return summed.astype(jnp.bfloat16)

    def home(virtual, micro):
        table = virtual * sections + micro
        starts = (section == 0) & (virtual == 0)
        ends = is_last & (virtual == 1)
        target = table + jnp.where(is_last, sections, 0)

        @pl.when(starts & (micro > 0))
        def _():
            settle(inbox.at[micro], inbox_sem.at[micro])

        @pl.when(jnp.logical_not(starts))
        def _():
            settle(stream_recv.at[table], stream_sem.at[table])
            settle(share_recv.at[table], share_sem.at[table])
            settle(back_recv.at[table], back_sem.at[table])

        current = jnp.where(starts, inbox[micro], combined(table))

        stream = current.astype(jnp.float32)
        mean_square = jnp.mean(stream * stream, axis=-1, keepdims=True)
        normed = stream * lax.rsqrt(mean_square + norm_epsilon) * gain_ref[virtual]
        normed = normed.astype(jnp.bfloat16)
        row_send[table] = blocks(
            jnp.dot(choose_ref[table], normed, preferred_element_type=jnp.float32)
        )
        for move in farthest[:-1]:
            to = chip(move)
            pltpu.make_async_remote_copy(
                row_send.at[table, to],
                row_recv.at[table, mine],
                row_send_sem.at[table],
                row_sem.at[table],
                device_id=(section, to * 2 + core),
                device_id_type=MESH,
            ).start()
        pltpu.make_async_copy(
            row_send.at[table, mine], row_recv.at[table, mine], row_sem.at[table]
        ).start()

        @pl.when(ends)
        def _():
            stream_recv[target] = current

        @pl.when(jnp.logical_not(ends))
        def _():
            stream_send[table] = current
            pltpu.make_async_remote_copy(
                stream_send.at[table],
                stream_recv.at[target],
                stream_send_sem.at[table],
                stream_sem.at[target],
                device_id=(following, place),
                device_id_type=MESH,
            ).start()

        logits = jnp.dot(normed, router_ref[virtual], preferred_element_type=jnp.float32)
        scores = mask_ref[table] / (1.0 + jnp.exp(-logits))
        lane = lax.broadcasted_iota(jnp.int32, scores.shape, 1)
        total = jnp.sum(jnp.where(lane >= EXPERT_LANE, scores, 0.0), axis=1, keepdims=True)
        share = jnp.where(lane < slots, scores / total, 0.0)
        high = share.astype(jnp.bfloat16)
        low = (share - high.astype(jnp.float32)).astype(jnp.bfloat16)
        pair = jnp.concatenate([high, low], axis=0)

        @pl.when(ends)
        def _():
            share_recv[target] = pair

        @pl.when(jnp.logical_not(ends))
        def _():
            share_send[table] = pair
            pltpu.make_async_remote_copy(
                share_send.at[table],
                share_recv.at[target],
                share_send_sem.at[table],
                share_sem.at[target],
                device_id=(following, place),
                device_id_type=MESH,
            ).start()

    def serve(virtual, micro):
        table = virtual * sections + micro
        two = lax.rem(micro, 2)
        ends = is_last & (virtual == 1)
        target = table + jnp.where(is_last, sections, 0)
        to_section = jnp.where(ends, section, following)

        settle(row_recv.at[table], row_sem.at[table])
        forward = pltpu.make_async_remote_copy(
            row_recv.at[table],
            pair_recv.at[two],
            pair_send_sem.at[two],
            pair_sem.at[two],
            device_id=(section, sibling),
            device_id_type=MESH,
        )
        forward.start()
        for early in range(2):

            @pl.when((micro == 0) & (virtual == early))
            def _(early=early):
                for load in loads[early]:
                    load.wait()

        def hidden_of(given):
            both = jnp.dot(given, gate_up[virtual], preferred_element_type=jnp.float32)
            gate_act, up_act = both[:, :ff], both[:, ff:]
            return (gate_act / (1.0 + jnp.exp(-gate_act)) * up_act).astype(jnp.bfloat16)

        def partial_of(hidden):
            return jnp.dot(
                hidden, down[virtual], preferred_element_type=jnp.float32
            ).astype(jnp.bfloat16)

        own_hidden = hidden_of(flat(row_recv[table]))
        forward.wait()
        half_send[two] = partial_of(hidden_of(flat(pair_recv[two])))
        half = pltpu.make_async_remote_copy(
            half_send.at[two],
            half_recv.at[two],
            half_send_sem.at[two],
            half_sem.at[two],
            device_id=(section, sibling),
            device_id_type=MESH,
        )
        half.start()
        own = partial_of(own_hidden).astype(jnp.float32)
        half.wait()
        back_send[table] = blocks(own + half_recv[two].astype(jnp.float32))

        def back_copy(to):
            return pltpu.make_async_remote_copy(
                back_send.at[table, to],
                back_recv.at[target, mine],
                back_send_sem.at[table],
                back_sem.at[target],
                device_id=(to_section, to * 2 + core),
                device_id_type=MESH,
            )

        for move in farthest[:-1]:
            back_copy(chip(move)).start()

        @pl.when(ends)
        def _():
            pltpu.make_async_copy(
                back_send.at[table, mine], back_recv.at[target, mine], back_sem.at[target]
            ).start()

        @pl.when(jnp.logical_not(ends))
        def _():
            back_copy(mine).start()

    def stage_copy(index):
        return pltpu.make_async_remote_copy(
            stage.at[index],
            final,
            stage_sem.at[index],
            final_sem,
            device_id=(index, place),
            device_id_type=MESH,
        )

    def finish(micro):
        slot = 2 * sections + micro
        settle(back_recv.at[slot], back_sem.at[slot])
        summed = combined(slot)

        @pl.when(micro == last_section)
        def _():
            final[...] = summed

        @pl.when(micro < last_section)
        def _():
            stage[micro] = summed
            stage_copy(micro).start()

    span = sections + LAG

    def turn(index, carry):
        virtual, step = lax.div(index, span), lax.rem(index, span)

        @pl.when(step < sections)
        def _():
            home(virtual, step)

        @pl.when(step >= LAG)
        def _():
            serve(virtual, step - LAG)

        return carry

    lax.fori_loop(0, 2 * span, turn, 0)

    @pl.when(is_last)
    def _():
        def finish_step(micro, carry):
            finish(micro)
            return carry

        lax.fori_loop(0, sections, finish_step, 0)
        for index in range(sections - 1):
            settle(stage.at[index], stage_sem.at[index])

    def drain(table, carry):
        ends = is_last & (table >= sections)
        settle(row_send.at[table, pl.ds(0, held - 1)], row_send_sem.at[table])
        settle(back_send.at[table, pl.ds(0, held - 1)], back_send_sem.at[table])

        @pl.when(jnp.logical_not(ends))
        def _():
            settle(back_send.at[table, held - 1], back_send_sem.at[table])
            settle(stream_send.at[table], stream_send_sem.at[table])
            settle(share_send.at[table], share_send_sem.at[table])

        return carry

    lax.fori_loop(0, 2 * sections, drain, 0)

    @pl.when(section > 0)
    def _():
        settle(tokens_ref, inbox_send_sem)

    @pl.when(section < last_section)
    def _():
        settle(final, final_sem)

    out_ref[...] = final[...]


def tables(ids, held):
    rows = ids.shape[-2]
    lane = jnp.arange(LANES, dtype=jnp.int32)
    slots = held * CAP
    meaning = jnp.where(
        lane < slots, lane // CAP, jnp.where(lane >= EXPERT_LANE, lane - EXPERT_LANE, -1)
    )
    named = jnp.any(ids[..., None] == meaning, axis=-2).astype(jnp.float32)
    row = jnp.arange(rows)
    earlier = (row[:, None] > row[None, :]).astype(jnp.float32)
    rank = jnp.sum(earlier[:, :, None] * named[:, None, :, :], axis=2)
    fits = (lane >= slots) | (rank == (lane % CAP).astype(jnp.float32))
    mask = named * fits.astype(jnp.float32)
    choose = jnp.swapaxes(mask[..., :slots], 1, 2).astype(jnp.bfloat16)
    return mask, choose


def body(tokens, expert_ids, norm_gain, router_weight, gate_weight, up_weight, down_weight):
    sections = lax.axis_size("section")
    held = lax.axis_size("expert") // 2
    rows, features = tokens.shape[1:]
    ff = gate_weight.shape[-1]
    slots = held * CAP
    experts = router_weight.shape[-1]
    mask, choose = tables(
        expert_ids[:, 0].reshape(-1, rows, expert_ids.shape[-1]), held
    )
    lane = jnp.arange(LANES, dtype=jnp.int32)
    meaning = jnp.where(
        lane < slots, lane // CAP, jnp.where(lane >= EXPERT_LANE, lane - EXPERT_LANE, -1)
    )
    spread = (jnp.arange(experts)[:, None] == meaning[None, :]).astype(jnp.bfloat16)
    router = jnp.dot(
        router_weight[:, 0], spread, preferred_element_type=jnp.float32
    ).astype(jnp.bfloat16)

    layers, arrivals = 2 * sections, 3 * sections
    bf16 = jnp.bfloat16
    dma = pltpu.SemaphoreType.DMA
    vmem = pl.BlockSpec(memory_space=pltpu.VMEM)
    hbm = pl.BlockSpec(memory_space=pltpu.HBM)
    block = (held, CAP, features)
    out = pl.pallas_call(
        functools.partial(relay_kernel, sections, held),
        out_shape=jax.ShapeDtypeStruct((rows, features), bf16),
        in_specs=[vmem] * 5 + [hbm] * 3,
        out_specs=vmem,
        scratch_shapes=[
            pltpu.VMEM((2, features, 2 * ff), bf16),
            pltpu.VMEM((2, ff, features), bf16),
            pltpu.VMEM((sections, rows, features), bf16),
            pltpu.VMEM((sections, rows, features), bf16),
            pltpu.VMEM((rows, features), bf16),
            pltpu.VMEM((layers, *block), bf16),
            pltpu.VMEM((layers, *block), bf16),
            pltpu.VMEM((2, *block), bf16),
            pltpu.VMEM((2, slots, features), bf16),
            pltpu.VMEM((2, slots, features), bf16),
            pltpu.VMEM((layers, *block), bf16),
            pltpu.VMEM((arrivals, *block), bf16),
            pltpu.VMEM((layers, rows, features), bf16),
            pltpu.VMEM((arrivals, rows, features), bf16),
            pltpu.VMEM((layers, 2 * rows, LANES), bf16),
            pltpu.VMEM((arrivals, 2 * rows, LANES), bf16),
            dma((2, 3)),
            dma,
            dma((sections,)),
            dma((sections,)),
            dma,
            dma((layers,)),
            dma((layers,)),
            dma((2,)),
            dma((2,)),
            dma((2,)),
            dma((2,)),
            dma((layers,)),
            dma((arrivals,)),
            dma((layers,)),
            dma((arrivals,)),
            dma((layers,)),
            dma((arrivals,)),
        ],
        compiler_params=pltpu.CompilerParams(
            collective_id=0, has_side_effects=True, vmem_limit_bytes=48 << 20
        ),
        name="relay",
    )(
        tokens[0],
        mask,
        choose,
        router,
        norm_gain.reshape(2, 1, features),
        gate_weight[:, 0, 0],
        up_weight[:, 0, 0],
        down_weight[:, 0, 0],
    )
    return out[None]


def solution(mesh):
    return jax.shard_map(
        body,
        mesh=mesh,
        in_specs=(
            P("section", "expert", None),
            P(None, "section", None, "expert", None),
            P(None, "section", None),
            P(None, "section", None, None),
            P(None, "section", "expert", None, None),
            P(None, "section", "expert", None, None),
            P(None, "section", "expert", None, None),
        ),
        out_specs=P("section", "expert", None),
        check_vma=False,
    )
```

```python
import functools

import jax
import jax.numpy as jnp
from jax import lax
from jax.experimental import pallas as pl
from jax.experimental.pallas import tpu as pltpu
from jax.sharding import PartitionSpec as P

CAP = 2
norm_epsilon = 1e-06

MESH = pl.DeviceIdType.MESH
LANES = 128
EXPERT_LANE = 64


def relay_kernel(
    sections,
    held,
    top,
    tokens_ref,
    ids_given,
    router_given,
    gain_given,
    gate_hbm,
    up_hbm,
    down_hbm,
    out_ref,
    gate_up,
    down,
    ids_ref,
    router_packed,
    router_ref,
    gain_ref,
    mask_ref,
    choose_ref,
    inbox,
    stage,
    final,
    row_send,
    row_recv,
    pair_recv,
    half_send,
    half_recv,
    back_send,
    back_recv,
    stream_send,
    stream_recv,
    share_send,
    share_recv,
    weight_sem,
    swap_send_sem,
    swap_sem,
    inbox_send_sem,
    inbox_sem,
    stage_sem,
    final_sem,
    row_send_sem,
    row_sem,
    pair_send_sem,
    pair_sem,
    half_send_sem,
    half_sem,
    back_send_sem,
    back_sem,
    stream_send_sem,
    stream_sem,
    share_send_sem,
    share_sem,
):
    section = lax.axis_index("section")
    place = lax.axis_index("expert")
    mine = lax.div(place, 2)
    core = lax.rem(place, 2)
    level, side = lax.div(mine, 2), lax.rem(mine, 2)
    levels = held // 2
    half = sections // 2
    last_section = sections - 1
    homed = lax.rem(section + half, sections)
    following = lax.rem(section + 1, sections)
    is_last = section == last_section
    homes_last = homed == last_section
    sibling = mine * 2 + 1 - core
    rows = tokens_ref.shape[0]
    slots = held * CAP
    ff = gate_hbm.shape[2]

    def flat(value):
        return value.reshape(slots, value.shape[-1])

    def blocks(value):
        return value.astype(jnp.bfloat16).reshape(held, CAP, value.shape[-1])

    farthest = sorted(
        ((up, across) for up in range(levels) for across in (1, 0)),
        key=lambda move: (-min(move[0], levels - move[0]), -move[1]),
    )

    def chip(move):
        up, across = move
        beside = 1 - side if across else side
        return lax.rem(level + up, levels) * 2 + beside

    def settle(ref, sem):
        pltpu.make_async_copy(ref, ref, sem).wait()

    loads = []
    for virtual in range(2):
        loads.append(
            [
                pltpu.make_async_copy(
                    gate_hbm.at[virtual],
                    gate_up.at[virtual, :, pl.ds(0, ff)],
                    weight_sem.at[virtual, 0],
                ),
                pltpu.make_async_copy(
                    up_hbm.at[virtual],
                    gate_up.at[virtual, :, pl.ds(ff, ff)],
                    weight_sem.at[virtual, 1],
                ),
                pltpu.make_async_copy(
                    down_hbm.at[virtual], down.at[virtual], weight_sem.at[virtual, 2]
                ),
            ]
        )
        for load in loads[-1]:
            load.start()

    barrier = pltpu.get_barrier_semaphore()
    greeted = 0

    def greet(to_section, to_place):
        pl.semaphore_signal(
            barrier, inc=1, device_id=(to_section, to_place), device_id_type=MESH
        )

    for ahead in range(sections):
        to_section = lax.rem(section + ahead, sections)
        if ahead in (half - 1, half, half + 1):

            def greet_step(step, carry, to_section=to_section):
                greet(to_section, lax.rem(mine + step, held) * 2 + core)
                return carry

            lax.fori_loop(0, held, greet_step, 0)
            greeted += held
        elif ahead:
            greet(to_section, place)
            greeted += 1
    greet(section, sibling)
    pl.semaphore_wait(barrier, greeted + 1)

    swaps = [
        pltpu.make_async_remote_copy(
            source,
            target,
            swap_send_sem.at[index],
            swap_sem.at[index],
            device_id=(homed, place),
            device_id_type=MESH,
        )
        for index, (source, target) in enumerate(
            (
                (ids_given, ids_ref),
                (gain_given, gain_ref),
                (router_given.at[0], router_packed.at[0]),
                (router_given.at[1], router_packed.at[1]),
            )
        )
    ]
    swaps[0].start()

    @pl.when(section != half)
    def _():
        pltpu.make_async_remote_copy(
            tokens_ref,
            inbox.at[section],
            inbox_send_sem,
            inbox_sem.at[section],
            device_id=(half, place),
            device_id_type=MESH,
        ).start()

    @pl.when(section == half)
    def _():
        inbox[half] = tokens_ref[...]

    for swap in swaps[1:]:
        swap.start()

    lane = lax.broadcasted_iota(jnp.int32, (rows, LANES), 1)

    def meaning_of(lanes):
        chosen = lax.shift_right_logical(lanes, 1)
        rest = jnp.where(lanes >= EXPERT_LANE, lanes - EXPERT_LANE, -1)
        return jnp.where(lanes < slots, chosen, rest)

    swaps[0].wait_recv()
    ids = ids_ref[...]
    meaning = meaning_of(lane)
    named = []
    for table in range(2 * sections):
        found = ids[:, table * top : table * top + 1] == meaning
        for pick in range(table * top + 1, table * top + top):
            found = found | (ids[:, pick : pick + 1] == meaning)
        named.append(jnp.where(found, 1.0, 0.0))
    triangle = lax.broadcasted_iota(jnp.int32, (rows, rows), 0) > lax.broadcasted_iota(
        jnp.int32, (rows, rows), 1
    )
    ranks = jnp.dot(
        jnp.where(triangle, 1.0, 0.0).astype(jnp.bfloat16),
        jnp.concatenate(named, axis=1).astype(jnp.bfloat16),
        preferred_element_type=jnp.float32,
    )
    parity = lax.rem(lane, CAP).astype(jnp.float32)
    for table in range(2 * sections):
        fits = (lane >= slots) | (ranks[:, table * LANES : (table + 1) * LANES] == parity)
        mask = jnp.where(fits, named[table], 0.0)
        mask_ref[table] = mask
        choose_ref[table] = jnp.transpose(mask)[:slots].astype(jnp.bfloat16)
    swaps[1].wait_recv()

    def expand_router(virtual):
        down_lanes = lax.broadcasted_iota(jnp.int32, (LANES, LANES), 0)
        wanted = meaning_of(lax.broadcasted_iota(jnp.int32, (LANES, LANES), 1))
        spread = jnp.concatenate(
            [
                jnp.where(down_lanes == wanted, 1.0, 0.0),
                jnp.where(down_lanes - EXPERT_LANE == wanted, 1.0, 0.0),
            ],
            axis=1,
        ).astype(jnp.bfloat16)
        wide = jnp.dot(
            router_packed[virtual], spread, preferred_element_type=jnp.float32
        ).astype(jnp.bfloat16)
        depth = wide.shape[0]
        router_ref[virtual, pl.ds(0, depth)] = wide[:, :LANES]
        router_ref[virtual, pl.ds(depth, depth)] = wide[:, LANES:]

    def combined(slot):
        added = jnp.dot(
            share_recv[slot][:, :slots],
            flat(back_recv[slot]),
            preferred_element_type=jnp.float32,
        )
        summed = stream_recv[slot].astype(jnp.float32) + (added[:rows] + added[rows:])
        return summed.astype(jnp.bfloat16)

    def home(virtual, micro):
        table = virtual * sections + micro
        starts = (homed == 0) & (virtual == 0)
        ends = homes_last & (virtual == 1)
        target = table + jnp.where(homes_last, sections, 0)

        @pl.when(starts & (micro != half))
        def _():
            settle(inbox.at[micro], inbox_sem.at[micro])

        @pl.when(jnp.logical_not(starts))
        def _():
            settle(stream_recv.at[table], stream_sem.at[table])
            settle(share_recv.at[table], share_sem.at[table])
            settle(back_recv.at[table], back_sem.at[table])

        current = jnp.where(starts, inbox[micro], combined(table))

        stream = current.astype(jnp.float32)
        mean_square = jnp.mean(stream * stream, axis=-1, keepdims=True)
        normed = stream * lax.rsqrt(mean_square + norm_epsilon) * gain_ref[virtual]
        normed = normed.astype(jnp.bfloat16)
        row_send[table] = blocks(
            jnp.dot(choose_ref[table], normed, preferred_element_type=jnp.float32)
        )
        for move in farthest:
            to = chip(move)
            pltpu.make_async_remote_copy(
                row_send.at[table, to],
                row_recv.at[table, mine],
                row_send_sem.at[table],
                row_sem.at[table],
                device_id=(homed, to * 2 + core),
                device_id_type=MESH,
            ).start()

        @pl.when(ends)
        def _():
            stream_recv[target] = current

        @pl.when(jnp.logical_not(ends))
        def _():
            stream_send[table] = current
            pltpu.make_async_remote_copy(
                stream_send.at[table],
                stream_recv.at[target],
                stream_send_sem.at[table],
                stream_sem.at[target],
                device_id=(following, place),
                device_id_type=MESH,
            ).start()

        for first in range(2):

            @pl.when((micro == 0) & (virtual == first))
            def _(first=first):
                swaps[2 + first].wait_recv()
                expand_router(first)

        logits = jnp.dot(normed, router_ref[virtual], preferred_element_type=jnp.float32)
        scores = mask_ref[table] / (1.0 + jnp.exp(-logits))
        total = jnp.sum(jnp.where(lane >= EXPERT_LANE, scores, 0.0), axis=1, keepdims=True)
        share = jnp.where(lane < slots, scores / total, 0.0)
        high = share.astype(jnp.bfloat16)
        low = (share - high.astype(jnp.float32)).astype(jnp.bfloat16)
        pair = jnp.concatenate([high, low], axis=0)

        @pl.when(ends)
        def _():
            share_recv[target] = pair

        @pl.when(jnp.logical_not(ends))
        def _():
            share_send[table] = pair
            pltpu.make_async_remote_copy(
                share_send.at[table],
                share_recv.at[target],
                share_send_sem.at[table],
                share_sem.at[target],
                device_id=(following, place),
                device_id_type=MESH,
            ).start()

    def serve(virtual, micro):
        table = virtual * sections + micro
        two = lax.rem(micro, 2)
        target = table + jnp.where(is_last, sections, 0)
        to_home = lax.rem(section + 1 + half, sections)
        to_home = jnp.where(is_last & (virtual == 1), last_section - half, to_home)

        settle(row_recv.at[table], row_sem.at[table])
        forward = pltpu.make_async_remote_copy(
            row_recv.at[table],
            pair_recv.at[two],
            pair_send_sem.at[two],
            pair_sem.at[two],
            device_id=(section, sibling),
            device_id_type=MESH,
        )
        forward.start()
        for early in range(2):

            @pl.when((micro == 0) & (virtual == early))
            def _(early=early):
                for load in loads[early]:
                    load.wait()

        def hidden_of(given):
            both = jnp.dot(given, gate_up[virtual], preferred_element_type=jnp.float32)
            gate_act, up_act = both[:, :ff], both[:, ff:]
            return (gate_act / (1.0 + jnp.exp(-gate_act)) * up_act).astype(jnp.bfloat16)

        def partial_of(hidden):
            return jnp.dot(
                hidden, down[virtual], preferred_element_type=jnp.float32
            ).astype(jnp.bfloat16)

        own_hidden = hidden_of(flat(row_recv[table]))
        forward.wait()
        half_send[two] = partial_of(hidden_of(flat(pair_recv[two])))
        exchange = pltpu.make_async_remote_copy(
            half_send.at[two],
            half_recv.at[two],
            half_send_sem.at[two],
            half_sem.at[two],
            device_id=(section, sibling),
            device_id_type=MESH,
        )
        exchange.start()
        own = partial_of(own_hidden).astype(jnp.float32)
        exchange.wait()
        back_send[table] = blocks(own + half_recv[two].astype(jnp.float32))

        for move in farthest:
            to = chip(move)
            pltpu.make_async_remote_copy(
                back_send.at[table, to],
                back_recv.at[target, mine],
                back_send_sem.at[table],
                back_sem.at[target],
                device_id=(to_home, to * 2 + core),
                device_id_type=MESH,
            ).start()

    def stage_copy(index):
        return pltpu.make_async_remote_copy(
            stage.at[index],
            final,
            stage_sem.at[index],
            final_sem,
            device_id=(index, place),
            device_id_type=MESH,
        )

    def finish(micro):
        slot = 2 * sections + micro
        settle(back_recv.at[slot], back_sem.at[slot])
        summed = combined(slot)

        @pl.when(micro == section)
        def _():
            final[...] = summed

        @pl.when(micro != section)
        def _():
            stage[micro] = summed
            stage_copy(micro).start()

    def turn(index, carry):
        phase, micro = lax.div(index, sections), lax.rem(index, sections)
        virtual = lax.div(phase, 2)
        at_home = (lax.rem(phase, 2) == 0) == (section >= half)

        @pl.when(at_home)
        def _():
            home(virtual, micro)

        @pl.when(jnp.logical_not(at_home))
        def _():
            serve(virtual, micro)

        return carry

    lax.fori_loop(0, 4 * sections, turn, 0)

    @pl.when(homes_last)
    def _():
        def finish_step(micro, carry):
            finish(micro)
            return carry

        lax.fori_loop(0, sections, finish_step, 0)

        def stage_drain(micro, carry):
            @pl.when(micro != section)
            def _():
                settle(stage.at[micro], stage_sem.at[micro])

            return carry

        lax.fori_loop(0, sections, stage_drain, 0)

    def drain(table, carry):
        settle(row_send.at[table], row_send_sem.at[table])
        settle(back_send.at[table], back_send_sem.at[table])

        @pl.when(jnp.logical_not(homes_last & (table >= sections)))
        def _():
            settle(stream_send.at[table], stream_send_sem.at[table])
            settle(share_send.at[table], share_send_sem.at[table])

        return carry

    lax.fori_loop(0, 2 * sections, drain, 0)
    for swap in swaps:
        swap.wait_send()

    @pl.when(section != half)
    def _():
        settle(tokens_ref, inbox_send_sem)

    @pl.when(jnp.logical_not(homes_last))
    def _():
        settle(final, final_sem)

    out_ref[...] = final[...]


def body(tokens, expert_ids, norm_gain, router_weight, gate_weight, up_weight, down_weight):
    sections = lax.axis_size("section")
    held = lax.axis_size("expert") // 2
    rows, features = tokens.shape[1:]
    ff = gate_weight.shape[-1]
    slots = held * CAP
    top = expert_ids.shape[-1]
    ids = expert_ids[:, 0].reshape(-1, rows, top)
    ids = jnp.swapaxes(ids, 0, 1).reshape(rows, -1)
    ids = jnp.pad(ids, ((0, 0), (0, LANES - ids.shape[1])))
    router = router_weight[:, 0]
    router = jnp.concatenate(
        [router[:, : features // 2], router[:, features // 2 :]], axis=-1
    )

    layers, arrivals = 2 * sections, 3 * sections
    bf16 = jnp.bfloat16
    dma = pltpu.SemaphoreType.DMA
    vmem = pl.BlockSpec(memory_space=pltpu.VMEM)
    hbm = pl.BlockSpec(memory_space=pltpu.HBM)
    block = (held, CAP, features)
    out = pl.pallas_call(
        functools.partial(relay_kernel, sections, held, top),
        out_shape=jax.ShapeDtypeStruct((rows, features), bf16),
        in_specs=[vmem] * 4 + [hbm] * 3,
        out_specs=vmem,
        scratch_shapes=[
            pltpu.VMEM((2, features, 2 * ff), bf16),
            pltpu.VMEM((2, ff, features), bf16),
            pltpu.VMEM((rows, LANES), jnp.int32),
            pltpu.VMEM((2, features // 2, LANES), bf16),
            pltpu.VMEM((2, features, LANES), bf16),
            pltpu.VMEM((2, 1, features), jnp.float32),
            pltpu.VMEM((layers, rows, LANES), jnp.float32),
            pltpu.VMEM((layers, slots, rows), bf16),
            pltpu.VMEM((sections, rows, features), bf16),
            pltpu.VMEM((sections, rows, features), bf16),
            pltpu.VMEM((rows, features), bf16),
            pltpu.VMEM((layers, *block), bf16),
            pltpu.VMEM((layers, *block), bf16),
            pltpu.VMEM((2, *block), bf16),
            pltpu.VMEM((2, slots, features), bf16),
            pltpu.VMEM((2, slots, features), bf16),
            pltpu.VMEM((layers, *block), bf16),
            pltpu.VMEM((arrivals, *block), bf16),
            pltpu.VMEM((layers, rows, features), bf16),
            pltpu.VMEM((arrivals, rows, features), bf16),
            pltpu.VMEM((layers, 2 * rows, LANES), bf16),
            pltpu.VMEM((arrivals, 2 * rows, LANES), bf16),
            dma((2, 3)),
            dma((4,)),
            dma((4,)),
            dma,
            dma((sections,)),
            dma((sections,)),
            dma,
            dma((layers,)),
            dma((layers,)),
            dma((2,)),
            dma((2,)),
            dma((2,)),
            dma((2,)),
            dma((layers,)),
            dma((arrivals,)),
            dma((layers,)),
            dma((arrivals,)),
            dma((layers,)),
            dma((arrivals,)),
        ],
        compiler_params=pltpu.CompilerParams(
            collective_id=0, has_side_effects=True, vmem_limit_bytes=48 << 20
        ),
        name="relay",
    )(
        tokens[0],
        ids,
        router,
        norm_gain.reshape(2, 1, features),
        gate_weight[:, 0, 0],
        up_weight[:, 0, 0],
        down_weight[:, 0, 0],
    )
    return out[None]


def solution(mesh):
    return jax.shard_map(
        body,
        mesh=mesh,
        in_specs=(
            P("section", "expert", None),
            P(None, "section", None, "expert", None),
            P(None, "section", None),
            P(None, "section", None, None),
            P(None, "section", "expert", None, None),
            P(None, "section", "expert", None, None),
            P(None, "section", "expert", None, None),
        ),
        out_specs=P("section", "expert", None),
        check_vma=False,
    )
```

```python
import functools

import jax
import jax.numpy as jnp
from jax import lax
from jax.experimental import pallas as pl
from jax.experimental.pallas import tpu as pltpu
from jax.sharding import PartitionSpec as P

CAP = 2
norm_epsilon = 1e-06

MESH = pl.DeviceIdType.MESH
LANES = 128
EXPERT_LANE = 64


def relay_kernel(
    sections,
    held,
    top,
    tokens_ref,
    ids_given,
    router_given,
    gain_given,
    gate_hbm,
    up_hbm,
    down_hbm,
    out_ref,
    gate_up,
    down,
    ids_ref,
    router_packed,
    router_ref,
    gain_ref,
    mask_ref,
    choose_ref,
    inbox,
    stage,
    final,
    row_send,
    row_recv,
    back_send,
    back_recv,
    stream_send,
    stream_recv,
    share_send,
    share_recv,
    weight_sem,
    lend_sem,
    borrow_sem,
    swap_send_sem,
    swap_sem,
    inbox_send_sem,
    inbox_sem,
    stage_sem,
    final_sem,
    row_send_sem,
    row_sem,
    back_send_sem,
    back_sem,
    stream_send_sem,
    stream_sem,
    share_send_sem,
    share_sem,
):
    section = lax.axis_index("section")
    place = lax.axis_index("expert")
    mine = lax.div(place, 2)
    core = lax.rem(place, 2)
    level, side = lax.div(mine, 2), lax.rem(mine, 2)
    levels = held // 2
    half = sections // 2
    last_section = sections - 1
    homed = lax.rem(section + half, sections)
    following = lax.rem(section + 1, sections)
    is_last = section == last_section
    homes_last = homed == last_section
    sibling = mine * 2 + 1 - core
    rows = tokens_ref.shape[0]
    slots = held * CAP
    ff = gate_hbm.shape[2]

    def flat(value):
        return value.reshape(slots, value.shape[-1])

    def blocks(value):
        return value.astype(jnp.bfloat16).reshape(held, CAP, value.shape[-1])

    farthest = sorted(
        ((up, across) for up in range(levels) for across in (1, 0)),
        key=lambda move: (-min(move[0], levels - move[0]), -move[1]),
    )

    def chip(move):
        up, across = move
        beside = 1 - side if across else side
        return lax.rem(level + up, levels) * 2 + beside

    def settle(ref, sem):
        pltpu.make_async_copy(ref, ref, sem).wait()

    def own_half(first):
        return pl.ds(pl.multiple_of(first + core * ff, LANES), ff)

    pieces = [
        [
            (gate_hbm.at[virtual], gate_up.at[virtual, :, own_half(0)]),
            (up_hbm.at[virtual], gate_up.at[virtual, :, own_half(2 * ff)]),
            (down_hbm.at[virtual], down.at[virtual, own_half(0)]),
        ]
        for virtual in range(2)
    ]
    loads = [
        [
            pltpu.make_async_copy(source, target, weight_sem.at[virtual, index])
            for index, (source, target) in enumerate(pieces[virtual])
        ]
        for virtual in range(2)
    ]
    lends = [
        [
            pltpu.make_async_remote_copy(
                source,
                target,
                lend_sem.at[virtual, index],
                borrow_sem.at[virtual, index],
                device_id=(section, sibling),
                device_id_type=MESH,
            )
            for index, (source, target) in enumerate(pieces[virtual])
        ]
        for virtual in range(2)
    ]
    for load in loads[0] + loads[1]:
        load.start()

    barrier = pltpu.get_barrier_semaphore()
    greeted = 0

    def greet(to_section, to_place):
        pl.semaphore_signal(
            barrier, inc=1, device_id=(to_section, to_place), device_id_type=MESH
        )

    for ahead in range(sections):
        to_section = lax.rem(section + ahead, sections)
        if ahead in (half - 1, half, half + 1):

            def greet_step(step, carry, to_section=to_section):
                greet(to_section, lax.rem(mine + step, held) * 2 + core)
                return carry

            lax.fori_loop(0, held, greet_step, 0)
            greeted += held
        elif ahead:
            greet(to_section, place)
            greeted += 1
    greet(section, sibling)
    pl.semaphore_wait(barrier, greeted + 1)

    swaps = [
        pltpu.make_async_remote_copy(
            source,
            target,
            swap_send_sem.at[index],
            swap_sem.at[index],
            device_id=(homed, place),
            device_id_type=MESH,
        )
        for index, (source, target) in enumerate(
            (
                (ids_given, ids_ref),
                (gain_given, gain_ref),
                (router_given.at[0], router_packed.at[0]),
                (router_given.at[1], router_packed.at[1]),
            )
        )
    ]
    swaps[0].start()

    @pl.when(section != half)
    def _():
        pltpu.make_async_remote_copy(
            tokens_ref,
            inbox.at[section],
            inbox_send_sem,
            inbox_sem.at[section],
            device_id=(half, place),
            device_id_type=MESH,
        ).start()

    @pl.when(section == half)
    def _():
        inbox[half] = tokens_ref[...]

    for swap in swaps[1:]:
        swap.start()

    for lend in lends[0] + lends[1]:
        lend.start()

    lane = lax.broadcasted_iota(jnp.int32, (rows, LANES), 1)

    def meaning_of(lanes):
        chosen = lax.shift_right_logical(lanes, 1)
        rest = jnp.where(lanes >= EXPERT_LANE, lanes - EXPERT_LANE, -1)
        return jnp.where(lanes < slots, chosen, rest)

    swaps[0].wait_recv()
    ids = ids_ref[...]
    meaning = meaning_of(lane)
    named = []
    for table in range(2 * sections):
        found = ids[:, table * top : table * top + 1] == meaning
        for pick in range(table * top + 1, table * top + top):
            found = found | (ids[:, pick : pick + 1] == meaning)
        named.append(jnp.where(found, 1.0, 0.0))
    triangle = lax.broadcasted_iota(jnp.int32, (rows, rows), 0) > lax.broadcasted_iota(
        jnp.int32, (rows, rows), 1
    )
    ranks = jnp.dot(
        jnp.where(triangle, 1.0, 0.0).astype(jnp.bfloat16),
        jnp.concatenate(named, axis=1).astype(jnp.bfloat16),
        preferred_element_type=jnp.float32,
    )
    parity = lax.rem(lane, CAP).astype(jnp.float32)
    for table in range(2 * sections):
        fits = (lane >= slots) | (ranks[:, table * LANES : (table + 1) * LANES] == parity)
        mask = jnp.where(fits, named[table], 0.0)
        mask_ref[table] = mask
        choose_ref[table] = jnp.transpose(mask)[:slots].astype(jnp.bfloat16)
    swaps[1].wait_recv()

    def expand_router(virtual):
        down_lanes = lax.broadcasted_iota(jnp.int32, (LANES, LANES), 0)
        wanted = meaning_of(lax.broadcasted_iota(jnp.int32, (LANES, LANES), 1))
        spread = jnp.concatenate(
            [
                jnp.where(down_lanes == wanted, 1.0, 0.0),
                jnp.where(down_lanes - EXPERT_LANE == wanted, 1.0, 0.0),
            ],
            axis=1,
        ).astype(jnp.bfloat16)
        wide = jnp.dot(
            router_packed[virtual], spread, preferred_element_type=jnp.float32
        ).astype(jnp.bfloat16)
        depth = wide.shape[0]
        router_ref[virtual, pl.ds(0, depth)] = wide[:, :LANES]
        router_ref[virtual, pl.ds(depth, depth)] = wide[:, LANES:]

    def combined(slot):
        added = jnp.dot(
            share_recv[slot][:, :slots],
            flat(back_recv[slot]),
            preferred_element_type=jnp.float32,
        )
        summed = stream_recv[slot].astype(jnp.float32) + (added[:rows] + added[rows:])
        return summed.astype(jnp.bfloat16)

    def home(virtual, micro):
        table = virtual * sections + micro
        starts = (homed == 0) & (virtual == 0)
        ends = homes_last & (virtual == 1)
        target = table + jnp.where(homes_last, sections, 0)

        @pl.when(starts & (micro != half))
        def _():
            settle(inbox.at[micro], inbox_sem.at[micro])

        @pl.when(jnp.logical_not(starts))
        def _():
            settle(stream_recv.at[table], stream_sem.at[table])
            settle(share_recv.at[table], share_sem.at[table])
            settle(back_recv.at[table], back_sem.at[table])

        current = jnp.where(starts, inbox[micro], combined(table))

        stream = current.astype(jnp.float32)
        mean_square = jnp.mean(stream * stream, axis=-1, keepdims=True)
        normed = stream * lax.rsqrt(mean_square + norm_epsilon) * gain_ref[virtual]
        normed = normed.astype(jnp.bfloat16)
        row_send[table] = blocks(
            jnp.dot(choose_ref[table], normed, preferred_element_type=jnp.float32)
        )
        for move in farthest:
            to = chip(move)
            pltpu.make_async_remote_copy(
                row_send.at[table, to],
                row_recv.at[table, mine],
                row_send_sem.at[table],
                row_sem.at[table],
                device_id=(homed, to * 2 + core),
                device_id_type=MESH,
            ).start()

        @pl.when(ends)
        def _():
            stream_recv[target] = current

        @pl.when(jnp.logical_not(ends))
        def _():
            stream_send[table] = current
            pltpu.make_async_remote_copy(
                stream_send.at[table],
                stream_recv.at[target],
                stream_send_sem.at[table],
                stream_sem.at[target],
                device_id=(following, place),
                device_id_type=MESH,
            ).start()

        for first in range(2):

            @pl.when((micro == 0) & (virtual == first))
            def _(first=first):
                swaps[2 + first].wait_recv()
                expand_router(first)

        logits = jnp.dot(normed, router_ref[virtual], preferred_element_type=jnp.float32)
        scores = mask_ref[table] / (1.0 + jnp.exp(-logits))
        total = jnp.sum(jnp.where(lane >= EXPERT_LANE, scores, 0.0), axis=1, keepdims=True)
        share = jnp.where(lane < slots, scores / total, 0.0)
        high = share.astype(jnp.bfloat16)
        low = (share - high.astype(jnp.float32)).astype(jnp.bfloat16)
        pair = jnp.concatenate([high, low], axis=0)

        @pl.when(ends)
        def _():
            share_recv[target] = pair

        @pl.when(jnp.logical_not(ends))
        def _():
            share_send[table] = pair
            pltpu.make_async_remote_copy(
                share_send.at[table],
                share_recv.at[target],
                share_send_sem.at[table],
                share_sem.at[target],
                device_id=(following, place),
                device_id_type=MESH,
            ).start()

    def serve(virtual, micro):
        table = virtual * sections + micro
        target = table + jnp.where(is_last, sections, 0)
        to_home = lax.rem(section + 1 + half, sections)
        to_home = jnp.where(is_last & (virtual == 1), last_section - half, to_home)

        settle(row_recv.at[table], row_sem.at[table])
        for early in range(2):

            @pl.when((micro == 0) & (virtual == early))
            def _(early=early):
                for load, lend in zip(loads[early], lends[early]):
                    load.wait()
                    lend.wait_recv()

        both = jnp.dot(
            flat(row_recv[table]), gate_up[virtual], preferred_element_type=jnp.float32
        )
        gate_act, up_act = both[:, : 2 * ff], both[:, 2 * ff :]
        hidden = (gate_act / (1.0 + jnp.exp(-gate_act)) * up_act).astype(jnp.bfloat16)
        back_send[table] = blocks(
            jnp.dot(hidden, down[virtual], preferred_element_type=jnp.float32)
        )

        for move in farthest:
            to = chip(move)
            pltpu.make_async_remote_copy(
                back_send.at[table, to],
                back_recv.at[target, mine],
                back_send_sem.at[table],
                back_sem.at[target],
                device_id=(to_home, to * 2 + core),
                device_id_type=MESH,
            ).start()

    def stage_copy(index):
        return pltpu.make_async_remote_copy(
            stage.at[index],
            final,
            stage_sem.at[index],
            final_sem,
            device_id=(index, place),
            device_id_type=MESH,
        )

    def finish(micro):
        slot = 2 * sections + micro
        settle(back_recv.at[slot], back_sem.at[slot])
        summed = combined(slot)

        @pl.when(micro == section)
        def _():
            final[...] = summed

        @pl.when(micro != section)
        def _():
            stage[micro] = summed
            stage_copy(micro).start()

    def turn(index, carry):
        phase, micro = lax.div(index, sections), lax.rem(index, sections)
        virtual = lax.div(phase, 2)
        at_home = (lax.rem(phase, 2) == 0) == (section >= half)

        @pl.when(at_home)
        def _():
            home(virtual, micro)

        @pl.when(jnp.logical_not(at_home))
        def _():
            serve(virtual, micro)

        return carry

    lax.fori_loop(0, 4 * sections, turn, 0)

    @pl.when(homes_last)
    def _():
        def finish_step(micro, carry):
            finish(micro)
            return carry

        lax.fori_loop(0, sections, finish_step, 0)

        def stage_drain(micro, carry):
            @pl.when(micro != section)
            def _():
                settle(stage.at[micro], stage_sem.at[micro])

            return carry

        lax.fori_loop(0, sections, stage_drain, 0)

    def drain(table, carry):
        settle(row_send.at[table], row_send_sem.at[table])
        settle(back_send.at[table], back_send_sem.at[table])

        @pl.when(jnp.logical_not(homes_last & (table >= sections)))
        def _():
            settle(stream_send.at[table], stream_send_sem.at[table])
            settle(share_send.at[table], share_send_sem.at[table])

        return carry

    lax.fori_loop(0, 2 * sections, drain, 0)
    for swap in swaps:
        swap.wait_send()

    @pl.when(section != half)
    def _():
        settle(tokens_ref, inbox_send_sem)

    @pl.when(jnp.logical_not(homes_last))
    def _():
        settle(final, final_sem)

    for lend in lends[0] + lends[1]:
        lend.wait_send()

    out_ref[...] = final[...]


def body(tokens, expert_ids, norm_gain, router_weight, gate_weight, up_weight, down_weight):
    sections = lax.axis_size("section")
    held = lax.axis_size("expert") // 2
    rows, features = tokens.shape[1:]
    ff = gate_weight.shape[-1]
    slots = held * CAP
    top = expert_ids.shape[-1]
    ids = expert_ids[:, 0].reshape(-1, rows, top)
    ids = jnp.swapaxes(ids, 0, 1).reshape(rows, -1)
    ids = jnp.pad(ids, ((0, 0), (0, LANES - ids.shape[1])))
    router = router_weight[:, 0]
    router = jnp.concatenate(
        [router[:, : features // 2], router[:, features // 2 :]], axis=-1
    )

    layers, arrivals = 2 * sections, 3 * sections
    bf16 = jnp.bfloat16
    dma = pltpu.SemaphoreType.DMA
    vmem = pl.BlockSpec(memory_space=pltpu.VMEM)
    hbm = pl.BlockSpec(memory_space=pltpu.HBM)
    block = (held, CAP, features)
    out = pl.pallas_call(
        functools.partial(relay_kernel, sections, held, top),
        out_shape=jax.ShapeDtypeStruct((rows, features), bf16),
        in_specs=[vmem] * 4 + [hbm] * 3,
        out_specs=vmem,
        scratch_shapes=[
            pltpu.VMEM((2, features, 4 * ff), bf16),
            pltpu.VMEM((2, 2 * ff, features), bf16),
            pltpu.VMEM((rows, LANES), jnp.int32),
            pltpu.VMEM((2, features // 2, LANES), bf16),
            pltpu.VMEM((2, features, LANES), bf16),
            pltpu.VMEM((2, 1, features), jnp.float32),
            pltpu.VMEM((layers, rows, LANES), jnp.float32),
            pltpu.VMEM((layers, slots, rows), bf16),
            pltpu.VMEM((sections, rows, features), bf16),
            pltpu.VMEM((sections, rows, features), bf16),
            pltpu.VMEM((rows, features), bf16),
            pltpu.VMEM((layers, *block), bf16),
            pltpu.VMEM((layers, *block), bf16),
            pltpu.VMEM((layers, *block), bf16),
            pltpu.VMEM((arrivals, *block), bf16),
            pltpu.VMEM((layers, rows, features), bf16),
            pltpu.VMEM((arrivals, rows, features), bf16),
            pltpu.VMEM((layers, 2 * rows, LANES), bf16),
            pltpu.VMEM((arrivals, 2 * rows, LANES), bf16),
            dma((2, 3)),
            dma((2, 3)),
            dma((2, 3)),
            dma((4,)),
            dma((4,)),
            dma,
            dma((sections,)),
            dma((sections,)),
            dma,
            dma((layers,)),
            dma((layers,)),
            dma((layers,)),
            dma((arrivals,)),
            dma((layers,)),
            dma((arrivals,)),
            dma((layers,)),
            dma((arrivals,)),
        ],
        compiler_params=pltpu.CompilerParams(
            collective_id=0, has_side_effects=True, vmem_limit_bytes=60 << 20
        ),
        name="relay",
    )(
        tokens[0],
        ids,
        router,
        norm_gain.reshape(2, 1, features),
        gate_weight[:, 0, 0],
        up_weight[:, 0, 0],
        down_weight[:, 0, 0],
    )
    return out[None]


def solution(mesh):
    return jax.shard_map(
        body,
        mesh=mesh,
        in_specs=(
            P("section", "expert", None),
            P(None, "section", None, "expert", None),
            P(None, "section", None),
            P(None, "section", None, None),
            P(None, "section", "expert", None, None),
            P(None, "section", "expert", None, None),
            P(None, "section", "expert", None, None),
        ),
        out_specs=P("section", "expert", None),
        check_vma=False,
    )
```

```python
import functools

import jax
import jax.numpy as jnp
from jax import lax
from jax.experimental import pallas as pl
from jax.experimental.pallas import tpu as pltpu
from jax.sharding import PartitionSpec as P

CAP = 2
norm_epsilon = 1e-06

MESH = pl.DeviceIdType.MESH
LANES = 128
EXPERT_LANE = 64


def relay_kernel(
    sections,
    held,
    top,
    tokens_ref,
    ids_given,
    router_given,
    gain_given,
    gate_hbm,
    up_hbm,
    down_hbm,
    out_ref,
    gate_up,
    down,
    ids_ref,
    router_packed,
    router_ref,
    gain_ref,
    mask_ref,
    choose_ref,
    inbox,
    stage,
    final,
    row_send,
    row_recv,
    back_send,
    back_recv,
    stream_send,
    stream_recv,
    share_send,
    share_recv,
    weight_sem,
    lend_sem,
    borrow_sem,
    swap_send_sem,
    swap_sem,
    inbox_send_sem,
    inbox_sem,
    stage_sem,
    final_sem,
    row_send_sem,
    row_sem,
    back_send_sem,
    back_sem,
    stream_send_sem,
    stream_sem,
    share_send_sem,
    share_sem,
):
    section = lax.axis_index("section")
    place = lax.axis_index("expert")
    mine = lax.div(place, 2)
    core = lax.rem(place, 2)
    level, side = lax.div(mine, 2), lax.rem(mine, 2)
    levels = held // 2
    half = sections // 2
    last_section = sections - 1
    homed = lax.rem(section + half, sections)
    following = lax.rem(section + 1, sections)
    is_last = section == last_section
    homes_last = homed == last_section
    sibling = mine * 2 + 1 - core
    rows = tokens_ref.shape[0]
    slots = held * CAP
    ff = gate_hbm.shape[2]

    def flat(value):
        return value.reshape(slots, value.shape[-1])

    def blocks(value):
        return value.astype(jnp.bfloat16).reshape(held, CAP, value.shape[-1])

    farthest = sorted(
        ((up, across) for up in range(levels) for across in (1, 0)),
        key=lambda move: (-min(move[0], levels - move[0]), -move[1]),
    )

    def chip(move):
        up, across = move
        beside = 1 - side if across else side
        return lax.rem(level + up, levels) * 2 + beside

    def settle(ref, sem):
        pltpu.make_async_copy(ref, ref, sem).wait()

    def own_half(first):
        return pl.ds(pl.multiple_of(first + core * ff, LANES), ff)

    pieces = [
        [
            (gate_hbm.at[virtual], gate_up.at[virtual, :, own_half(0)]),
            (up_hbm.at[virtual], gate_up.at[virtual, :, own_half(2 * ff)]),
            (down_hbm.at[virtual], down.at[virtual, own_half(0)]),
        ]
        for virtual in range(2)
    ]
    loads = [
        [
            pltpu.make_async_copy(source, target, weight_sem.at[virtual, index])
            for index, (source, target) in enumerate(pieces[virtual])
        ]
        for virtual in range(2)
    ]
    lends = [
        [
            pltpu.make_async_remote_copy(
                source,
                target,
                lend_sem.at[virtual, index],
                borrow_sem.at[virtual, index],
                device_id=(section, sibling),
                device_id_type=MESH,
            )
            for index, (source, target) in enumerate(pieces[virtual])
        ]
        for virtual in range(2)
    ]
    for load in loads[0]:
        load.start()

    barrier = pltpu.get_barrier_semaphore()
    greeted = 0

    def greet(to_section, to_place):
        pl.semaphore_signal(
            barrier, inc=1, device_id=(to_section, to_place), device_id_type=MESH
        )

    for ahead in range(1, sections):
        greet(lax.rem(section + ahead, sections), place)
        greeted += 1
    greet(section, sibling)
    greeted += 1

    @pl.when(section == 0)
    def _():
        def greet_step(step, carry):
            greet(half, lax.rem(mine + step, held) * 2 + core)
            return carry

        lax.fori_loop(1, held, greet_step, 0)

    pl.semaphore_wait(barrier, jnp.where(section == half, greeted + held - 1, greeted))

    swaps = [
        pltpu.make_async_remote_copy(
            source,
            target,
            swap_send_sem.at[index],
            swap_sem.at[index],
            device_id=(homed, place),
            device_id_type=MESH,
        )
        for index, (source, target) in enumerate(
            (
                (ids_given, ids_ref),
                (gain_given, gain_ref),
                (router_given.at[0], router_packed.at[0]),
                (router_given.at[1], router_packed.at[1]),
            )
        )
    ]
    swaps[0].start()

    @pl.when(section != half)
    def _():
        pltpu.make_async_remote_copy(
            tokens_ref,
            inbox.at[section],
            inbox_send_sem,
            inbox_sem.at[section],
            device_id=(half, place),
            device_id_type=MESH,
        ).start()

    @pl.when(section == half)
    def _():
        inbox[half] = tokens_ref[...]

    for swap in swaps[1:]:
        swap.start()

    @pl.when(section < half)
    def _():
        for lend in lends[0]:
            lend.start()

    lane = lax.broadcasted_iota(jnp.int32, (rows, LANES), 1)

    def meaning_of(lanes):
        chosen = lax.shift_right_logical(lanes, 1)
        rest = jnp.where(lanes >= EXPERT_LANE, lanes - EXPERT_LANE, -1)
        return jnp.where(lanes < slots, chosen, rest)

    swaps[0].wait_recv()
    ids = ids_ref[...]
    meaning = meaning_of(lane)
    named = []
    for table in range(2 * sections):
        found = ids[:, table * top : table * top + 1] == meaning
        for pick in range(table * top + 1, table * top + top):
            found = found | (ids[:, pick : pick + 1] == meaning)
        named.append(jnp.where(found, 1.0, 0.0))
    triangle = lax.broadcasted_iota(jnp.int32, (rows, rows), 0) > lax.broadcasted_iota(
        jnp.int32, (rows, rows), 1
    )
    ranks = jnp.dot(
        jnp.where(triangle, 1.0, 0.0).astype(jnp.bfloat16),
        jnp.concatenate(named, axis=1).astype(jnp.bfloat16),
        preferred_element_type=jnp.float32,
    )
    parity = lax.rem(lane, CAP).astype(jnp.float32)
    for table in range(2 * sections):
        fits = (lane >= slots) | (ranks[:, table * LANES : (table + 1) * LANES] == parity)
        mask = jnp.where(fits, named[table], 0.0)
        mask_ref[table] = mask
        choose_ref[table] = jnp.transpose(mask)[:slots].astype(jnp.bfloat16)
    swaps[1].wait_recv()

    def expand_router(virtual):
        experts = router_packed.shape[1]
        wanted = meaning_of(lax.broadcasted_iota(jnp.int32, (LANES, experts), 0))
        spread = lax.broadcasted_iota(jnp.int32, (LANES, experts), 1) == wanted
        router_ref[virtual] = jnp.dot(
            jnp.where(spread, 1.0, 0.0).astype(jnp.bfloat16),
            router_packed[virtual],
            preferred_element_type=jnp.float32,
        ).astype(jnp.bfloat16)

    def combined(slot):
        added = jnp.dot(
            share_recv[slot][:, :slots],
            flat(back_recv[slot]),
            preferred_element_type=jnp.float32,
        )
        summed = stream_recv[slot].astype(jnp.float32) + (added[:rows] + added[rows:])
        return summed.astype(jnp.bfloat16)

    def home(virtual, micro):
        table = virtual * sections + micro
        starts = (homed == 0) & (virtual == 0)
        ends = homes_last & (virtual == 1)
        target = table + jnp.where(homes_last, sections, 0)

        @pl.when(starts & (micro != half))
        def _():
            settle(inbox.at[micro], inbox_sem.at[micro])

        @pl.when(jnp.logical_not(starts))
        def _():
            settle(stream_recv.at[table], stream_sem.at[table])
            settle(share_recv.at[table], share_sem.at[table])
            settle(back_recv.at[table], back_sem.at[table])

        current = jnp.where(starts, inbox[micro], combined(table))

        stream = current.astype(jnp.float32)
        mean_square = jnp.mean(stream * stream, axis=-1, keepdims=True)
        normed = stream * lax.rsqrt(mean_square + norm_epsilon) * gain_ref[virtual]
        normed = normed.astype(jnp.bfloat16)
        row_send[table] = blocks(
            jnp.dot(choose_ref[table], normed, preferred_element_type=jnp.float32)
        )
        for move in farthest:
            to = chip(move)
            pltpu.make_async_remote_copy(
                row_send.at[table, to],
                row_recv.at[table, mine],
                row_send_sem.at[table],
                row_sem.at[table],
                device_id=(homed, to * 2 + core),
                device_id_type=MESH,
            ).start()

        @pl.when(ends)
        def _():
            stream_recv[target] = current

        @pl.when(jnp.logical_not(ends))
        def _():
            stream_send[table] = current
            pltpu.make_async_remote_copy(
                stream_send.at[table],
                stream_recv.at[target],
                stream_send_sem.at[table],
                stream_sem.at[target],
                device_id=(following, place),
                device_id_type=MESH,
            ).start()

        for first in range(2):

            @pl.when((micro == 0) & (virtual == first))
            def _(first=first):
                swaps[2 + first].wait_recv()
                expand_router(first)

        logits = lax.dot_general(
            normed,
            router_ref[virtual],
            (((1,), (1,)), ((), ())),
            preferred_element_type=jnp.float32,
        )
        scores = mask_ref[table] / (1.0 + jnp.exp(-logits))
        total = jnp.sum(jnp.where(lane >= EXPERT_LANE, scores, 0.0), axis=1, keepdims=True)
        share = jnp.where(lane < slots, scores / total, 0.0)
        high = share.astype(jnp.bfloat16)
        low = (share - high.astype(jnp.float32)).astype(jnp.bfloat16)
        pair = jnp.concatenate([high, low], axis=0)

        @pl.when(ends)
        def _():
            share_recv[target] = pair

        @pl.when(jnp.logical_not(ends))
        def _():
            share_send[table] = pair
            pltpu.make_async_remote_copy(
                share_send.at[table],
                share_recv.at[target],
                share_send_sem.at[table],
                share_sem.at[target],
                device_id=(following, place),
                device_id_type=MESH,
            ).start()

    def serve(virtual, micro):
        table = virtual * sections + micro
        target = table + jnp.where(is_last, sections, 0)
        to_home = lax.rem(section + 1 + half, sections)
        to_home = jnp.where(is_last & (virtual == 1), last_section - half, to_home)

        settle(row_recv.at[table], row_sem.at[table])
        def arrive(pieces_used):
            for early in range(2):

                @pl.when((micro == 0) & (virtual == early))
                def _(early=early):
                    for index in pieces_used:
                        loads[early][index].wait()
                        lends[early][index].wait_recv()

        arrive((0, 1))
        both = jnp.dot(
            flat(row_recv[table]), gate_up[virtual], preferred_element_type=jnp.float32
        )
        gate_act, up_act = both[:, : 2 * ff], both[:, 2 * ff :]
        hidden = (gate_act / (1.0 + jnp.exp(-gate_act)) * up_act).astype(jnp.bfloat16)
        arrive((2,))
        back_send[table] = blocks(
            jnp.dot(hidden, down[virtual], preferred_element_type=jnp.float32)
        )

        for move in farthest:
            to = chip(move)
            pltpu.make_async_remote_copy(
                back_send.at[table, to],
                back_recv.at[target, mine],
                back_send_sem.at[table],
                back_sem.at[target],
                device_id=(to_home, to * 2 + core),
                device_id_type=MESH,
            ).start()

    def stage_copy(index):
        return pltpu.make_async_remote_copy(
            stage.at[index],
            final,
            stage_sem.at[index],
            final_sem,
            device_id=(index, place),
            device_id_type=MESH,
        )

    def finish(micro):
        slot = 2 * sections + micro
        settle(back_recv.at[slot], back_sem.at[slot])
        summed = combined(slot)

        @pl.when(micro == section)
        def _():
            final[...] = summed

        @pl.when(micro != section)
        def _():
            stage[micro] = summed
            stage_copy(micro).start()

    def turn(index, carry):
        phase, micro = lax.div(index, sections), lax.rem(index, sections)
        virtual = lax.div(phase, 2)
        at_home = (lax.rem(phase, 2) == 0) == (section >= half)

        @pl.when(index == sections)
        def _():
            for load, lend in zip(loads[1], lends[1]):
                load.start()
                lend.start()

        @pl.when(at_home)
        def _():
            home(virtual, micro)

            @pl.when((section >= half) & (index == 0))
            def _():
                for lend in lends[0]:
                    lend.start()

        @pl.when(jnp.logical_not(at_home))
        def _():
            serve(virtual, micro)

        return carry

    lax.fori_loop(0, 4 * sections, turn, 0)

    @pl.when(homes_last)
    def _():
        def finish_step(micro, carry):
            finish(micro)
            return carry

        lax.fori_loop(0, sections, finish_step, 0)

        def stage_drain(micro, carry):
            @pl.when(micro != section)
            def _():
                settle(stage.at[micro], stage_sem.at[micro])

            return carry

        lax.fori_loop(0, sections, stage_drain, 0)

    def drain(table, carry):
        settle(row_send.at[table], row_send_sem.at[table])
        settle(back_send.at[table], back_send_sem.at[table])

        @pl.when(jnp.logical_not(homes_last & (table >= sections)))
        def _():
            settle(stream_send.at[table], stream_send_sem.at[table])
            settle(share_send.at[table], share_send_sem.at[table])

        return carry

    lax.fori_loop(0, 2 * sections, drain, 0)
    for swap in swaps:
        swap.wait_send()

    @pl.when(section != half)
    def _():
        settle(tokens_ref, inbox_send_sem)

    @pl.when(jnp.logical_not(homes_last))
    def _():
        settle(final, final_sem)

    for lend in lends[0] + lends[1]:
        lend.wait_send()

    out_ref[...] = final[...]


def body(tokens, expert_ids, norm_gain, router_weight, gate_weight, up_weight, down_weight):
    sections = lax.axis_size("section")
    held = lax.axis_size("expert") // 2
    rows, features = tokens.shape[1:]
    ff = gate_weight.shape[-1]
    slots = held * CAP
    top = expert_ids.shape[-1]
    ids = expert_ids[:, 0].reshape(-1, rows, top)
    ids = jnp.swapaxes(ids, 0, 1).reshape(rows, -1)
    ids = jnp.pad(ids, ((0, 0), (0, LANES - ids.shape[1])))
    router = jnp.swapaxes(router_weight[:, 0], 1, 2)

    layers, arrivals = 2 * sections, 3 * sections
    bf16 = jnp.bfloat16
    dma = pltpu.SemaphoreType.DMA
    vmem = pl.BlockSpec(memory_space=pltpu.VMEM)
    hbm = pl.BlockSpec(memory_space=pltpu.HBM)
    block = (held, CAP, features)
    out = pl.pallas_call(
        functools.partial(relay_kernel, sections, held, top),
        out_shape=jax.ShapeDtypeStruct((rows, features), bf16),
        in_specs=[vmem] * 4 + [hbm] * 3,
        out_specs=vmem,
        scratch_shapes=[
            pltpu.VMEM((2, features, 4 * ff), bf16),
            pltpu.VMEM((2, 2 * ff, features), bf16),
            pltpu.VMEM((rows, LANES), jnp.int32),
            pltpu.VMEM((2, router.shape[1], features), bf16),
            pltpu.VMEM((2, LANES, features), bf16),
            pltpu.VMEM((2, 1, features), jnp.float32),
            pltpu.VMEM((layers, rows, LANES), jnp.float32),
            pltpu.VMEM((layers, slots, rows), bf16),
            pltpu.VMEM((sections, rows, features), bf16),
            pltpu.VMEM((sections, rows, features), bf16),
            pltpu.VMEM((rows, features), bf16),
            pltpu.VMEM((layers, *block), bf16),
            pltpu.VMEM((layers, *block), bf16),
            pltpu.VMEM((layers, *block), bf16),
            pltpu.VMEM((arrivals, *block), bf16),
            pltpu.VMEM((layers, rows, features), bf16),
            pltpu.VMEM((arrivals, rows, features), bf16),
            pltpu.VMEM((layers, 2 * rows, LANES), bf16),
            pltpu.VMEM((arrivals, 2 * rows, LANES), bf16),
            dma((2, 3)),
            dma((2, 3)),
            dma((2, 3)),
            dma((4,)),
            dma((4,)),
            dma,
            dma((sections,)),
            dma((sections,)),
            dma,
            dma((layers,)),
            dma((layers,)),
            dma((layers,)),
            dma((arrivals,)),
            dma((layers,)),
            dma((arrivals,)),
            dma((layers,)),
            dma((arrivals,)),
        ],
        compiler_params=pltpu.CompilerParams(
            collective_id=0, has_side_effects=True, vmem_limit_bytes=60 << 20
        ),
        name="relay",
    )(
        tokens[0],
        ids,
        router,
        norm_gain.reshape(2, 1, features),
        gate_weight[:, 0, 0],
        up_weight[:, 0, 0],
        down_weight[:, 0, 0],
    )
    return out[None]


def solution(mesh):
    return jax.shard_map(
        body,
        mesh=mesh,
        in_specs=(
            P("section", "expert", None),
            P(None, "section", None, "expert", None),
            P(None, "section", None),
            P(None, "section", None, None),
            P(None, "section", "expert", None, None),
            P(None, "section", "expert", None, None),
            P(None, "section", "expert", None, None),
        ),
        out_specs=P("section", "expert", None),
        check_vma=False,
    )
```

```python
import functools

import jax
import jax.numpy as jnp
from jax import lax
from jax.experimental import pallas as pl
from jax.experimental.pallas import tpu as pltpu
from jax.sharding import PartitionSpec as P

CAP = 2
norm_epsilon = 1e-06

MESH = pl.DeviceIdType.MESH
LANES = 128
EXPERT_LANE = 64


def relay_kernel(
    sections,
    held,
    top,
    tokens_ref,
    ids_given,
    router_given,
    gain_given,
    gate_hbm,
    up_hbm,
    down_hbm,
    out_ref,
    gate_up,
    down,
    ids_ref,
    router_packed,
    router_ref,
    gain_ref,
    mask_ref,
    choose_ref,
    inbox,
    stage,
    final,
    row_send,
    row_recv,
    back_send,
    back_recv,
    stream_send,
    stream_recv,
    share_send,
    share_recv,
    weight_sem,
    lend_sem,
    borrow_sem,
    swap_send_sem,
    swap_sem,
    inbox_send_sem,
    inbox_sem,
    stage_sem,
    final_sem,
    row_send_sem,
    row_sem,
    back_send_sem,
    back_sem,
    stream_send_sem,
    stream_sem,
    share_send_sem,
    share_sem,
):
    section = lax.axis_index("section")
    place = lax.axis_index("expert")
    mine = lax.div(place, 2)
    core = lax.rem(place, 2)
    level, side = lax.div(mine, 2), lax.rem(mine, 2)
    levels = held // 2
    half = sections // 2
    last_section = sections - 1
    homed = lax.rem(section + half, sections)
    following = lax.rem(section + 1, sections)
    is_last = section == last_section
    homes_last = homed == last_section
    sibling = mine * 2 + 1 - core
    rows = tokens_ref.shape[0]
    slots = held * CAP
    ff = gate_hbm.shape[2]

    def flat(value):
        return value.reshape(slots, value.shape[-1])

    def blocks(value):
        return value.astype(jnp.bfloat16).reshape(held, CAP, value.shape[-1])

    farthest = sorted(
        ((up, across) for up in range(levels) for across in (1, 0)),
        key=lambda move: (-min(move[0], levels - move[0]), -move[1]),
    )

    def chip(move):
        up, across = move
        beside = 1 - side if across else side
        return lax.rem(level + up, levels) * 2 + beside

    def settle(ref, sem):
        pltpu.make_async_copy(ref, ref, sem).wait()

    def own_half(first):
        return pl.ds(pl.multiple_of(first + core * ff, LANES), ff)

    pieces = [
        [
            (gate_hbm.at[virtual], gate_up.at[virtual, :, own_half(0)]),
            (up_hbm.at[virtual], gate_up.at[virtual, :, own_half(2 * ff)]),
            (down_hbm.at[virtual], down.at[virtual, own_half(0)]),
        ]
        for virtual in range(2)
    ]
    loads = [
        [
            pltpu.make_async_copy(source, target, weight_sem.at[virtual, index])
            for index, (source, target) in enumerate(pieces[virtual])
        ]
        for virtual in range(2)
    ]
    lends = [
        [
            pltpu.make_async_remote_copy(
                source,
                target,
                lend_sem.at[virtual, index],
                borrow_sem.at[virtual, index],
                device_id=(section, sibling),
                device_id_type=MESH,
            )
            for index, (source, target) in enumerate(pieces[virtual])
        ]
        for virtual in range(2)
    ]
    for load in loads[0]:
        load.start()

    barrier = pltpu.get_barrier_semaphore()
    greeted = 0

    def greet(to_section, to_place):
        pl.semaphore_signal(
            barrier, inc=1, device_id=(to_section, to_place), device_id_type=MESH
        )

    for ahead in range(1, sections):
        greet(lax.rem(section + ahead, sections), place)
        greeted += 1
    greet(section, sibling)
    greeted += 1

    @pl.when(section == 0)
    def _():
        def greet_step(step, carry):
            greet(half, lax.rem(mine + step, held) * 2 + core)
            return carry

        lax.fori_loop(1, held, greet_step, 0)

    pl.semaphore_wait(barrier, jnp.where(section == half, greeted + held - 1, greeted))

    swaps = [
        pltpu.make_async_remote_copy(
            source,
            target,
            swap_send_sem.at[index],
            swap_sem.at[index],
            device_id=(homed, place),
            device_id_type=MESH,
        )
        for index, (source, target) in enumerate(
            (
                (ids_given, ids_ref),
                (gain_given, gain_ref),
                (router_given.at[0], router_packed.at[0]),
                (router_given.at[1], router_packed.at[1]),
            )
        )
    ]
    swaps[0].start()

    @pl.when(section != half)
    def _():
        pltpu.make_async_remote_copy(
            tokens_ref,
            inbox.at[section],
            inbox_send_sem,
            inbox_sem.at[section],
            device_id=(half, place),
            device_id_type=MESH,
        ).start()

    @pl.when(section == half)
    def _():
        inbox[half] = tokens_ref[...]

    for swap in swaps[1:]:
        swap.start()

    @pl.when(section < half)
    def _():
        for lend in lends[0]:
            lend.start()

    lane = lax.broadcasted_iota(jnp.int32, (rows, LANES), 1)

    def meaning_of(lanes):
        chosen = lax.shift_right_logical(lanes, 1)
        rest = jnp.where(lanes >= EXPERT_LANE, lanes - EXPERT_LANE, -1)
        return jnp.where(lanes < slots, chosen, rest)

    swaps[0].wait_recv()
    ids = ids_ref[...]
    meaning = meaning_of(lane)
    named = []
    for table in range(2 * sections):
        found = ids[:, table * top : table * top + 1] == meaning
        for pick in range(table * top + 1, table * top + top):
            found = found | (ids[:, pick : pick + 1] == meaning)
        named.append(jnp.where(found, 1.0, 0.0))
    triangle = lax.broadcasted_iota(jnp.int32, (rows, rows), 0) > lax.broadcasted_iota(
        jnp.int32, (rows, rows), 1
    )
    ranks = jnp.dot(
        jnp.where(triangle, 1.0, 0.0).astype(jnp.bfloat16),
        jnp.concatenate(named, axis=1).astype(jnp.bfloat16),
        preferred_element_type=jnp.float32,
    )
    parity = lax.rem(lane, CAP).astype(jnp.float32)
    for table in range(2 * sections):
        fits = (lane >= slots) | (ranks[:, table * LANES : (table + 1) * LANES] == parity)
        mask = jnp.where(fits, named[table], 0.0)
        mask_ref[table] = mask
        choose_ref[table] = jnp.transpose(mask)[:slots].astype(jnp.bfloat16)
    swaps[1].wait_recv()

    def expand_router(virtual):
        experts = router_packed.shape[1]
        wanted = meaning_of(lax.broadcasted_iota(jnp.int32, (LANES, experts), 0))
        spread = lax.broadcasted_iota(jnp.int32, (LANES, experts), 1) == wanted
        router_ref[virtual] = jnp.dot(
            jnp.where(spread, 1.0, 0.0).astype(jnp.bfloat16),
            router_packed[virtual],
            preferred_element_type=jnp.float32,
        ).astype(jnp.bfloat16)

    def combined(slot):
        added = jnp.dot(
            share_recv[slot][:, :slots],
            flat(back_recv[slot]),
            preferred_element_type=jnp.float32,
        )
        summed = stream_recv[slot].astype(jnp.float32) + (added[:rows] + added[rows:])
        return summed.astype(jnp.bfloat16)

    def home(virtual, micro):
        table = virtual * sections + micro
        starts = (homed == 0) & (virtual == 0)
        ends = homes_last & (virtual == 1)
        target = table + jnp.where(homes_last, sections, 0)

        @pl.when(starts & (micro != half))
        def _():
            settle(inbox.at[micro], inbox_sem.at[micro])

        @pl.when(jnp.logical_not(starts))
        def _():
            settle(stream_recv.at[table], stream_sem.at[table])
            settle(share_recv.at[table], share_sem.at[table])
            settle(back_recv.at[table], back_sem.at[table])

        current = jnp.where(starts, inbox[micro], combined(table))

        stream = current.astype(jnp.float32)
        mean_square = jnp.mean(stream * stream, axis=-1, keepdims=True)
        normed = stream * lax.rsqrt(mean_square + norm_epsilon) * gain_ref[virtual]
        normed = normed.astype(jnp.bfloat16)
        row_send[table] = blocks(
            jnp.dot(choose_ref[table], normed, preferred_element_type=jnp.float32)
        )
        @pl.when(starts & (micro > 0))
        def _():
            settle(row_send.at[table - 1], row_send_sem.at[table - 1])

        for move in farthest:
            to = chip(move)
            pltpu.make_async_remote_copy(
                row_send.at[table, to],
                row_recv.at[table, mine],
                row_send_sem.at[table],
                row_sem.at[table],
                device_id=(homed, to * 2 + core),
                device_id_type=MESH,
            ).start()

        @pl.when(ends)
        def _():
            stream_recv[target] = current

        @pl.when(jnp.logical_not(ends))
        def _():
            stream_send[table] = current
            pltpu.make_async_remote_copy(
                stream_send.at[table],
                stream_recv.at[target],
                stream_send_sem.at[table],
                stream_sem.at[target],
                device_id=(following, place),
                device_id_type=MESH,
            ).start()

        for first in range(2):

            @pl.when((micro == 0) & (virtual == first))
            def _(first=first):
                swaps[2 + first].wait_recv()
                expand_router(first)

        logits = lax.dot_general(
            normed,
            router_ref[virtual],
            (((1,), (1,)), ((), ())),
            preferred_element_type=jnp.float32,
        )
        scores = mask_ref[table] / (1.0 + jnp.exp(-logits))
        total = jnp.sum(jnp.where(lane >= EXPERT_LANE, scores, 0.0), axis=1, keepdims=True)
        share = jnp.where(lane < slots, scores / total, 0.0)
        high = share.astype(jnp.bfloat16)
        low = (share - high.astype(jnp.float32)).astype(jnp.bfloat16)
        pair = jnp.concatenate([high, low], axis=0)

        @pl.when(ends)
        def _():
            share_recv[target] = pair

        @pl.when(jnp.logical_not(ends))
        def _():
            share_send[table] = pair
            pltpu.make_async_remote_copy(
                share_send.at[table],
                share_recv.at[target],
                share_send_sem.at[table],
                share_sem.at[target],
                device_id=(following, place),
                device_id_type=MESH,
            ).start()

    def serve(virtual, micro):
        table = virtual * sections + micro
        target = table + jnp.where(is_last, sections, 0)
        to_home = lax.rem(section + 1 + half, sections)
        to_home = jnp.where(is_last & (virtual == 1), last_section - half, to_home)

        settle(row_recv.at[table], row_sem.at[table])
        def arrive(pieces_used):
            for early in range(2):

                @pl.when((micro == 0) & (virtual == early))
                def _(early=early):
                    for index in pieces_used:
                        loads[early][index].wait()
                        lends[early][index].wait_recv()

        arrive((0, 1))
        both = jnp.dot(
            flat(row_recv[table]), gate_up[virtual], preferred_element_type=jnp.float32
        )
        gate_act, up_act = both[:, : 2 * ff], both[:, 2 * ff :]
        hidden = (gate_act / (1.0 + jnp.exp(-gate_act)) * up_act).astype(jnp.bfloat16)
        arrive((2,))
        back_send[table] = blocks(
            jnp.dot(hidden, down[virtual], preferred_element_type=jnp.float32)
        )

        for move in farthest:
            to = chip(move)
            pltpu.make_async_remote_copy(
                back_send.at[table, to],
                back_recv.at[target, mine],
                back_send_sem.at[table],
                back_sem.at[target],
                device_id=(to_home, to * 2 + core),
                device_id_type=MESH,
            ).start()

    def stage_copy(index):
        return pltpu.make_async_remote_copy(
            stage.at[index],
            final,
            stage_sem.at[index],
            final_sem,
            device_id=(index, place),
            device_id_type=MESH,
        )

    def finish(micro):
        slot = 2 * sections + micro
        settle(back_recv.at[slot], back_sem.at[slot])
        summed = combined(slot)

        @pl.when(micro == section)
        def _():
            final[...] = summed

        @pl.when(micro != section)
        def _():
            stage[micro] = summed
            stage_copy(micro).start()

    def turn(index, carry):
        phase, micro = lax.div(index, sections), lax.rem(index, sections)
        virtual = lax.div(phase, 2)
        at_home = (lax.rem(phase, 2) == 0) == (section >= half)

        @pl.when(index == sections)
        def _():
            for load, lend in zip(loads[1], lends[1]):
                load.start()
                lend.start()

        @pl.when(at_home)
        def _():
            home(virtual, micro)

            @pl.when((section >= half) & (index == 0))
            def _():
                for lend in lends[0]:
                    lend.start()

        @pl.when(jnp.logical_not(at_home))
        def _():
            serve(virtual, micro)

        return carry

    lax.fori_loop(0, 4 * sections, turn, 0)

    @pl.when(homes_last)
    def _():
        def finish_step(micro, carry):
            finish(micro)
            return carry

        lax.fori_loop(0, sections, finish_step, 0)

        def stage_drain(micro, carry):
            @pl.when(micro != section)
            def _():
                settle(stage.at[micro], stage_sem.at[micro])

            return carry

        lax.fori_loop(0, sections, stage_drain, 0)

    def drain(table, carry):
        @pl.when((homed > 0) | (table >= sections - 1))
        def _():
            settle(row_send.at[table], row_send_sem.at[table])

        settle(back_send.at[table], back_send_sem.at[table])

        @pl.when(jnp.logical_not(homes_last & (table >= sections)))
        def _():
            settle(stream_send.at[table], stream_send_sem.at[table])
            settle(share_send.at[table], share_send_sem.at[table])

        return carry

    lax.fori_loop(0, 2 * sections, drain, 0)
    for swap in swaps:
        swap.wait_send()

    @pl.when(section != half)
    def _():
        settle(tokens_ref, inbox_send_sem)

    @pl.when(jnp.logical_not(homes_last))
    def _():
        settle(final, final_sem)

    for lend in lends[0] + lends[1]:
        lend.wait_send()

    out_ref[...] = final[...]


def body(tokens, expert_ids, norm_gain, router_weight, gate_weight, up_weight, down_weight):
    sections = lax.axis_size("section")
    held = lax.axis_size("expert") // 2
    rows, features = tokens.shape[1:]
    ff = gate_weight.shape[-1]
    slots = held * CAP
    top = expert_ids.shape[-1]
    ids = expert_ids[:, 0].reshape(-1, rows, top)
    ids = jnp.swapaxes(ids, 0, 1).reshape(rows, -1)
    ids = jnp.pad(ids, ((0, 0), (0, LANES - ids.shape[1])))
    router = jnp.swapaxes(router_weight[:, 0], 1, 2)

    layers, arrivals = 2 * sections, 3 * sections
    bf16 = jnp.bfloat16
    dma = pltpu.SemaphoreType.DMA
    vmem = pl.BlockSpec(memory_space=pltpu.VMEM)
    hbm = pl.BlockSpec(memory_space=pltpu.HBM)
    block = (held, CAP, features)
    out = pl.pallas_call(
        functools.partial(relay_kernel, sections, held, top),
        out_shape=jax.ShapeDtypeStruct((rows, features), bf16),
        in_specs=[vmem] * 4 + [hbm] * 3,
        out_specs=vmem,
        scratch_shapes=[
            pltpu.VMEM((2, features, 4 * ff), bf16),
            pltpu.VMEM((2, 2 * ff, features), bf16),
            pltpu.VMEM((rows, LANES), jnp.int32),
            pltpu.VMEM((2, router.shape[1], features), bf16),
            pltpu.VMEM((2, LANES, features), bf16),
            pltpu.VMEM((2, 1, features), jnp.float32),
            pltpu.VMEM((layers, rows, LANES), jnp.float32),
            pltpu.VMEM((layers, slots, rows), bf16),
            pltpu.VMEM((sections, rows, features), bf16),
            pltpu.VMEM((sections, rows, features), bf16),
            pltpu.VMEM((rows, features), bf16),
            pltpu.VMEM((layers, *block), bf16),
            pltpu.VMEM((layers, *block), bf16),
            pltpu.VMEM((layers, *block), bf16),
            pltpu.VMEM((arrivals, *block), bf16),
            pltpu.VMEM((layers, rows, features), bf16),
            pltpu.VMEM((arrivals, rows, features), bf16),
            pltpu.VMEM((layers, 2 * rows, LANES), bf16),
            pltpu.VMEM((arrivals, 2 * rows, LANES), bf16),
            dma((2, 3)),
            dma((2, 3)),
            dma((2, 3)),
            dma((4,)),
            dma((4,)),
            dma,
            dma((sections,)),
            dma((sections,)),
            dma,
            dma((layers,)),
            dma((layers,)),
            dma((layers,)),
            dma((arrivals,)),
            dma((layers,)),
            dma((arrivals,)),
            dma((layers,)),
            dma((arrivals,)),
        ],
        compiler_params=pltpu.CompilerParams(
            collective_id=0, has_side_effects=True, vmem_limit_bytes=60 << 20
        ),
        name="relay",
    )(
        tokens[0],
        ids,
        router,
        norm_gain.reshape(2, 1, features),
        gate_weight[:, 0, 0],
        up_weight[:, 0, 0],
        down_weight[:, 0, 0],
    )
    return out[None]


def solution(mesh):
    return jax.shard_map(
        body,
        mesh=mesh,
        in_specs=(
            P("section", "expert", None),
            P(None, "section", None, "expert", None),
            P(None, "section", None),
            P(None, "section", None, None),
            P(None, "section", "expert", None, None),
            P(None, "section", "expert", None, None),
            P(None, "section", "expert", None, None),
        ),
        out_specs=P("section", "expert", None),
        check_vma=False,
    )
```

```python
import functools

import jax
import jax.numpy as jnp
from jax import lax
from jax.experimental import pallas as pl
from jax.experimental.pallas import tpu as pltpu
from jax.sharding import PartitionSpec as P

CAP = 2
norm_epsilon = 1e-06

MESH = pl.DeviceIdType.MESH
LANES = 128
EXPERT_LANE = 64


def relay_kernel(
    sections,
    held,
    top,
    tokens_ref,
    ids_given,
    router_given,
    gain_given,
    gate_hbm,
    up_hbm,
    down_hbm,
    out_ref,
    gate_up,
    down,
    ids_ref,
    router_packed,
    router_ref,
    gain_ref,
    mask_ref,
    choose_ref,
    inbox,
    stage,
    final,
    row_send,
    row_recv,
    back_send,
    back_recv,
    stream_send,
    stream_recv,
    share_send,
    share_recv,
    weight_sem,
    lend_sem,
    borrow_sem,
    swap_send_sem,
    swap_sem,
    inbox_send_sem,
    inbox_sem,
    stage_sem,
    final_sem,
    row_send_sem,
    row_sem,
    back_send_sem,
    back_sem,
    stream_send_sem,
    stream_sem,
    share_send_sem,
    share_sem,
):
    section = lax.axis_index("section")
    place = lax.axis_index("expert")
    mine = lax.div(place, 2)
    core = lax.rem(place, 2)
    level, side = lax.div(mine, 2), lax.rem(mine, 2)
    levels = held // 2
    half = sections // 2
    last_section = sections - 1
    homed = lax.rem(section + half, sections)
    following = lax.rem(section + 1, sections)
    is_last = section == last_section
    homes_last = homed == last_section
    sibling = mine * 2 + 1 - core
    rows = tokens_ref.shape[0]
    slots = held * CAP
    ff = gate_hbm.shape[2]

    def flat(value):
        return value.reshape(slots, value.shape[-1])

    def blocks(value):
        return value.astype(jnp.bfloat16).reshape(held, CAP, value.shape[-1])

    farthest = sorted(
        ((up, across) for up in range(levels) for across in (1, 0)),
        key=lambda move: (-min(move[0], levels - move[0]), -move[1]),
    )

    def chip(move):
        up, across = move
        beside = 1 - side if across else side
        return lax.rem(level + up, levels) * 2 + beside

    def settle(ref, sem):
        pltpu.make_async_copy(ref, ref, sem).wait()

    def own_half(first):
        return pl.ds(pl.multiple_of(first + core * ff, LANES), ff)

    pieces = [
        [
            (gate_hbm.at[virtual], gate_up.at[virtual, :, own_half(0)]),
            (up_hbm.at[virtual], gate_up.at[virtual, :, own_half(2 * ff)]),
            (down_hbm.at[virtual], down.at[virtual, own_half(0)]),
        ]
        for virtual in range(2)
    ]
    loads = [
        [
            pltpu.make_async_copy(source, target, weight_sem.at[virtual, index])
            for index, (source, target) in enumerate(pieces[virtual])
        ]
        for virtual in range(2)
    ]
    lends = [
        [
            pltpu.make_async_remote_copy(
                source,
                target,
                lend_sem.at[virtual, index],
                borrow_sem.at[virtual, index],
                device_id=(section, sibling),
                device_id_type=MESH,
            )
            for index, (source, target) in enumerate(pieces[virtual])
        ]
        for virtual in range(2)
    ]
    for load in loads[0]:
        load.start()

    barrier = pltpu.get_barrier_semaphore()
    greeted = 0

    def greet(to_section, to_place):
        pl.semaphore_signal(
            barrier, inc=1, device_id=(to_section, to_place), device_id_type=MESH
        )

    for ahead in range(1, sections):
        greet(lax.rem(section + ahead, sections), place)
        greeted += 1
    greet(section, sibling)
    greeted += 1

    @pl.when(section == 0)
    def _():
        def greet_step(step, carry):
            greet(half, lax.rem(mine + step, held) * 2 + core)
            return carry

        lax.fori_loop(1, held, greet_step, 0)

    pl.semaphore_wait(barrier, jnp.where(section == half, greeted + held - 1, greeted))

    swaps = [
        pltpu.make_async_remote_copy(
            source,
            target,
            swap_send_sem.at[index],
            swap_sem.at[index],
            device_id=(homed, place),
            device_id_type=MESH,
        )
        for index, (source, target) in enumerate(
            (
                (ids_given, ids_ref),
                (gain_given, gain_ref),
                (router_given.at[0], router_packed.at[0]),
                (router_given.at[1], router_packed.at[1]),
            )
        )
    ]
    swaps[0].start()

    @pl.when(section != half)
    def _():
        pltpu.make_async_remote_copy(
            tokens_ref,
            inbox.at[section],
            inbox_send_sem,
            inbox_sem.at[section],
            device_id=(half, place),
            device_id_type=MESH,
        ).start()

    @pl.when(section == half)
    def _():
        inbox[half] = tokens_ref[...]

    for swap in swaps[1:]:
        swap.start()

    @pl.when(section < half)
    def _():
        for lend in lends[0]:
            lend.start()

    lane = lax.broadcasted_iota(jnp.int32, (rows, LANES), 1)

    def meaning_of(lanes):
        chosen = lax.shift_right_logical(lanes, 1)
        rest = jnp.where(lanes >= EXPERT_LANE, lanes - EXPERT_LANE, -1)
        return jnp.where(lanes < slots, chosen, rest)

    swaps[0].wait_recv()
    ids = ids_ref[...]
    meaning = meaning_of(lane)
    named = []
    for table in range(2 * sections):
        found = ids[:, table * top : table * top + 1] == meaning
        for pick in range(table * top + 1, table * top + top):
            found = found | (ids[:, pick : pick + 1] == meaning)
        named.append(jnp.where(found, 1.0, 0.0))
    triangle = lax.broadcasted_iota(jnp.int32, (rows, rows), 0) > lax.broadcasted_iota(
        jnp.int32, (rows, rows), 1
    )
    ranks = jnp.dot(
        jnp.where(triangle, 1.0, 0.0).astype(jnp.bfloat16),
        jnp.concatenate(named, axis=1).astype(jnp.bfloat16),
        preferred_element_type=jnp.float32,
    )
    parity = lax.rem(lane, CAP).astype(jnp.float32)
    for table in range(2 * sections):
        fits = (lane >= slots) | (ranks[:, table * LANES : (table + 1) * LANES] == parity)
        mask = jnp.where(fits, named[table], 0.0)
        mask_ref[table] = mask
        choose_ref[table] = jnp.transpose(mask)[:slots].astype(jnp.bfloat16)
    swaps[1].wait_recv()

    def expand_router(virtual):
        experts = router_packed.shape[1]
        wanted = meaning_of(lax.broadcasted_iota(jnp.int32, (LANES, experts), 0))
        spread = lax.broadcasted_iota(jnp.int32, (LANES, experts), 1) == wanted
        router_ref[virtual] = jnp.dot(
            jnp.where(spread, 1.0, 0.0).astype(jnp.bfloat16),
            router_packed[virtual],
            preferred_element_type=jnp.float32,
        ).astype(jnp.bfloat16)

    def combined(slot):
        added = jnp.dot(
            share_recv[slot][:, :slots],
            flat(back_recv[slot]),
            preferred_element_type=jnp.float32,
        )
        summed = stream_recv[slot].astype(jnp.float32) + (added[:rows] + added[rows:])
        return summed.astype(jnp.bfloat16)

    def home(virtual, micro):
        table = virtual * sections + micro
        starts = (homed == 0) & (virtual == 0)
        ends = homes_last & (virtual == 1)
        target = table + jnp.where(homes_last, sections, 0)

        @pl.when(starts & (micro != half))
        def _():
            settle(inbox.at[micro], inbox_sem.at[micro])

        @pl.when(jnp.logical_not(starts))
        def _():
            settle(stream_recv.at[table], stream_sem.at[table])
            settle(share_recv.at[table], share_sem.at[table])
            settle(back_recv.at[table], back_sem.at[table])

        current = jnp.where(starts, inbox[micro], combined(table))

        stream = current.astype(jnp.float32)
        mean_square = jnp.mean(stream * stream, axis=-1, keepdims=True)
        normed = stream * lax.rsqrt(mean_square + norm_epsilon) * gain_ref[virtual]
        normed = normed.astype(jnp.bfloat16)
        row_send[table] = blocks(
            jnp.dot(choose_ref[table], normed, preferred_element_type=jnp.float32)
        )
        @pl.when(starts & (micro > 0))
        def _():
            settle(row_send.at[table - 1], row_send_sem.at[table - 1])

        for move in farthest:
            to = chip(move)
            pltpu.make_async_remote_copy(
                row_send.at[table, to],
                row_recv.at[table, mine],
                row_send_sem.at[table],
                row_sem.at[table],
                device_id=(homed, to * 2 + core),
                device_id_type=MESH,
            ).start()

        beyond = jnp.where(ends, homed, following)
        stream_send[table] = current
        pltpu.make_async_remote_copy(
            stream_send.at[table],
            stream_recv.at[target],
            stream_send_sem.at[table],
            stream_sem.at[target],
            device_id=(beyond, place),
            device_id_type=MESH,
        ).start()

        for first in range(2):

            @pl.when((micro == 0) & (virtual == first))
            def _(first=first):
                swaps[2 + first].wait_recv()
                expand_router(first)

        logits = lax.dot_general(
            normed,
            router_ref[virtual],
            (((1,), (1,)), ((), ())),
            preferred_element_type=jnp.float32,
        )
        scores = mask_ref[table] / (1.0 + jnp.exp(-logits))
        total = jnp.sum(jnp.where(lane >= EXPERT_LANE, scores, 0.0), axis=1, keepdims=True)
        share = jnp.where(lane < slots, scores / total, 0.0)
        high = share.astype(jnp.bfloat16)
        low = (share - high.astype(jnp.float32)).astype(jnp.bfloat16)
        share_send[table] = jnp.concatenate([high, low], axis=0)
        pltpu.make_async_remote_copy(
            share_send.at[table],
            share_recv.at[target],
            share_send_sem.at[table],
            share_sem.at[target],
            device_id=(beyond, place),
            device_id_type=MESH,
        ).start()

    def serve(virtual, micro):
        table = virtual * sections + micro
        target = table + jnp.where(is_last, sections, 0)
        to_home = lax.rem(section + 1 + half, sections)
        ends = is_last & (virtual == 1)
        to_home = jnp.where(ends, section, to_home)

        settle(row_recv.at[table], row_sem.at[table])
        def arrive(pieces_used):
            for early in range(2):

                @pl.when((micro == 0) & (virtual == early))
                def _(early=early):
                    for index in pieces_used:
                        loads[early][index].wait()
                        lends[early][index].wait_recv()

        arrive((0, 1))
        both = jnp.dot(
            flat(row_recv[table]), gate_up[virtual], preferred_element_type=jnp.float32
        )
        gate_act, up_act = both[:, : 2 * ff], both[:, 2 * ff :]
        hidden = (gate_act / (1.0 + jnp.exp(-gate_act)) * up_act).astype(jnp.bfloat16)
        arrive((2,))
        back_send[table] = blocks(
            jnp.dot(hidden, down[virtual], preferred_element_type=jnp.float32)
        )

        def back_copy(to):
            return pltpu.make_async_remote_copy(
                back_send.at[table, to],
                back_recv.at[target, mine],
                back_send_sem.at[table],
                back_sem.at[target],
                device_id=(to_home, to * 2 + core),
                device_id_type=MESH,
            )

        for move in farthest[:-1]:
            back_copy(chip(move)).start()

        @pl.when(ends)
        def _():
            pltpu.make_async_copy(
                back_send.at[table, mine], back_recv.at[target, mine], back_sem.at[target]
            ).start()

        @pl.when(jnp.logical_not(ends))
        def _():
            back_copy(mine).start()

    def stage_copy(index):
        return pltpu.make_async_remote_copy(
            stage.at[index],
            final,
            stage_sem.at[index],
            final_sem,
            device_id=(index, place),
            device_id_type=MESH,
        )

    def finish(micro):
        slot = 2 * sections + micro
        settle(stream_recv.at[slot], stream_sem.at[slot])
        settle(share_recv.at[slot], share_sem.at[slot])
        settle(back_recv.at[slot], back_sem.at[slot])
        summed = combined(slot)

        @pl.when(micro == section)
        def _():
            final[...] = summed

        @pl.when(micro != section)
        def _():
            stage[micro] = summed
            stage_copy(micro).start()

    def turn(index, carry):
        phase, micro = lax.div(index, sections), lax.rem(index, sections)
        virtual = lax.div(phase, 2)
        at_home = (lax.rem(phase, 2) == 0) == (section >= half)

        @pl.when(index == sections)
        def _():
            for load, lend in zip(loads[1], lends[1]):
                load.start()
                lend.start()

        @pl.when(at_home)
        def _():
            home(virtual, micro)

            @pl.when((section >= half) & (index == 0))
            def _():
                for lend in lends[0]:
                    lend.start()

        @pl.when(jnp.logical_not(at_home))
        def _():
            serve(virtual, micro)

        return carry

    lax.fori_loop(0, 4 * sections, turn, 0)

    @pl.when(is_last)
    def _():
        def finish_step(micro, carry):
            finish(micro)
            return carry

        lax.fori_loop(0, sections, finish_step, 0)

        def stage_drain(micro, carry):
            @pl.when(micro != section)
            def _():
                settle(stage.at[micro], stage_sem.at[micro])

            return carry

        lax.fori_loop(0, sections, stage_drain, 0)

    def drain(table, carry):
        @pl.when((homed > 0) | (table >= sections - 1))
        def _():
            settle(row_send.at[table], row_send_sem.at[table])

        settle(back_send.at[table, pl.ds(0, held - 1)], back_send_sem.at[table])
        settle(stream_send.at[table], stream_send_sem.at[table])
        settle(share_send.at[table], share_send_sem.at[table])

        @pl.when(jnp.logical_not(is_last & (table >= sections)))
        def _():
            settle(back_send.at[table, held - 1], back_send_sem.at[table])

        return carry

    lax.fori_loop(0, 2 * sections, drain, 0)
    for swap in swaps:
        swap.wait_send()

    @pl.when(section != half)
    def _():
        settle(tokens_ref, inbox_send_sem)

    @pl.when(jnp.logical_not(is_last))
    def _():
        settle(final, final_sem)

    for lend in lends[0] + lends[1]:
        lend.wait_send()

    out_ref[...] = final[...]


def body(tokens, expert_ids, norm_gain, router_weight, gate_weight, up_weight, down_weight):
    sections = lax.axis_size("section")
    held = lax.axis_size("expert") // 2
    rows, features = tokens.shape[1:]
    ff = gate_weight.shape[-1]
    slots = held * CAP
    top = expert_ids.shape[-1]
    ids = expert_ids[:, 0].reshape(-1, rows, top)
    ids = jnp.swapaxes(ids, 0, 1).reshape(rows, -1)
    ids = jnp.pad(ids, ((0, 0), (0, LANES - ids.shape[1])))
    router = jnp.swapaxes(router_weight[:, 0], 1, 2)

    layers, arrivals = 2 * sections, 3 * sections
    bf16 = jnp.bfloat16
    dma = pltpu.SemaphoreType.DMA
    vmem = pl.BlockSpec(memory_space=pltpu.VMEM)
    hbm = pl.BlockSpec(memory_space=pltpu.HBM)
    block = (held, CAP, features)
    out = pl.pallas_call(
        functools.partial(relay_kernel, sections, held, top),
        out_shape=jax.ShapeDtypeStruct((rows, features), bf16),
        in_specs=[vmem] * 4 + [hbm] * 3,
        out_specs=vmem,
        scratch_shapes=[
            pltpu.VMEM((2, features, 4 * ff), bf16),
            pltpu.VMEM((2, 2 * ff, features), bf16),
            pltpu.VMEM((rows, LANES), jnp.int32),
            pltpu.VMEM((2, router.shape[1], features), bf16),
            pltpu.VMEM((2, LANES, features), bf16),
            pltpu.VMEM((2, 1, features), jnp.float32),
            pltpu.VMEM((layers, rows, LANES), jnp.float32),
            pltpu.VMEM((layers, slots, rows), bf16),
            pltpu.VMEM((sections, rows, features), bf16),
            pltpu.VMEM((sections, rows, features), bf16),
            pltpu.VMEM((rows, features), bf16),
            pltpu.VMEM((layers, *block), bf16),
            pltpu.VMEM((layers, *block), bf16),
            pltpu.VMEM((layers, *block), bf16),
            pltpu.VMEM((arrivals, *block), bf16),
            pltpu.VMEM((layers, rows, features), bf16),
            pltpu.VMEM((arrivals, rows, features), bf16),
            pltpu.VMEM((layers, 2 * rows, LANES), bf16),
            pltpu.VMEM((arrivals, 2 * rows, LANES), bf16),
            dma((2, 3)),
            dma((2, 3)),
            dma((2, 3)),
            dma((4,)),
            dma((4,)),
            dma,
            dma((sections,)),
            dma((sections,)),
            dma,
            dma((layers,)),
            dma((layers,)),
            dma((layers,)),
            dma((arrivals,)),
            dma((layers,)),
            dma((arrivals,)),
            dma((layers,)),
            dma((arrivals,)),
        ],
        compiler_params=pltpu.CompilerParams(
            collective_id=0, has_side_effects=True, vmem_limit_bytes=60 << 20
        ),
        name="relay",
    )(
        tokens[0],
        ids,
        router,
        norm_gain.reshape(2, 1, features),
        gate_weight[:, 0, 0],
        up_weight[:, 0, 0],
        down_weight[:, 0, 0],
    )
    return out[None]


def solution(mesh):
    return jax.shard_map(
        body,
        mesh=mesh,
        in_specs=(
            P("section", "expert", None),
            P(None, "section", None, "expert", None),
            P(None, "section", None),
            P(None, "section", None, None),
            P(None, "section", "expert", None, None),
            P(None, "section", "expert", None, None),
            P(None, "section", "expert", None, None),
        ),
        out_specs=P("section", "expert", None),
        check_vma=False,
    )
```
